512 devices in a mesh: row: 32 (over x_lo, z), col: 16 (over y, x_hi, core).
Axes of the slice: x: 4 (x_hi: 2, x_lo: 2; x = x_hi * 2 + x_lo), y: 4, z: 16, core: 2. Of those that a mesh axis runs over, the one named last changes fastest.
Arguments:
- snapshots: float32 [65536, 4096], P('row', 'col'), may hold values from -260 to 260
Outputs:
- rotated: float32 [65536, 4096], P('row', 'col')
The draws below stay inside these ranges and needn't reach their ends.
All inputs are finite; a program needn't handle non-finite values.
Results may differ from the reference program's by a relative error of at most 0.0003.
Values sent between devices are 32-bit elements; how exact they have to be, the bound alone decides.
A program may use at most 64 MiB of HBM per device.

```python
import jax
import jax.numpy as jnp
import numpy as np
from jax import lax

BLOCK = 128
INNER_ROUNDS = 10
ROWS = 65536
NCOL = 4096


def draw_snapshots(key, part):
    key_base = jax.random.fold_in(key, 11)
    key_cols = jax.random.fold_in(key, 12)
    base = jnp.clip(jax.random.normal(key_base, (ROWS, NCOL), jnp.float32), -6.0, 6.0)
    col_scale = jnp.exp(jax.random.uniform(key_cols, (NCOL,), jnp.float32, 0.0, jnp.log(10.0)))
    values = base * col_scale[None, :]
    return values.astype(jnp.float32)


def setup_inputs(seed: int = 0) -> dict:
    key_of = jax.random.split(jax.random.key(seed), 2)
    return {
        "snapshots": draw_snapshots(jax.random.fold_in(key_of[1], 71), 0),
    }


def round_tables(width, count):
    partner = np.zeros((count, width), np.int32)
    first = np.zeros((count, width), np.bool_)
    for turn in range(count):
        start = turn % (width - 1)
        pairs = [(start, width - 1)]
        for step in range(1, width // 2):
            pairs.append(((start + step) % (width - 1), (start - step) % (width - 1)))
        for left, right in pairs:
            lower, upper = min(left, right), max(left, right)
            partner[turn, lower] = upper
            partner[turn, upper] = lower
            first[turn, lower] = True
    return partner, first


def jacobi(gram, count):
    width = gram.shape[0]
    partner_np, first_np = round_tables(width, count)
    partner = jnp.asarray(partner_np)
    first = jnp.asarray(first_np)

    def turn(index, state):
        matrix, basis = state
        other = partner[index]
        lead = first[index]
        diag = jnp.diagonal(matrix)
        diag_other = jnp.take(diag, other)
        cross = jnp.take_along_axis(matrix, other[:, None], axis=1)[:, 0]
        gamma = jnp.where(lead, cross, jnp.take(cross, other))
        gap = jnp.where(lead, diag - diag_other, diag_other - diag)
        sigma = jnp.where(gap >= 0, 1.0, -1.0).astype(matrix.dtype)
        theta = 0.5 * jnp.arctan2(-2.0 * gamma * sigma, jnp.abs(gap))
        cosine = jnp.cos(theta)
        sine = jnp.sin(theta)
        factor = jnp.where(lead, -sine, sine)
        matrix = matrix * cosine[None, :] + jnp.take(matrix, other, axis=1) * factor[None, :]
        matrix = cosine[:, None] * matrix + factor[:, None] * jnp.take(matrix, other, axis=0)
        basis = basis * cosine[None, :] + jnp.take(basis, other, axis=1) * factor[None, :]
        return matrix, basis

    start = (gram, jnp.eye(width, dtype=gram.dtype))
    matrix, basis = lax.fori_loop(0, count, turn, start)
    return basis


def dot_high(left, right):
    return jnp.dot(left, right, precision=lax.Precision.HIGHEST, preferred_element_type=jnp.float32)


def pair_step(blocks):
    top, bottom = blocks
    half = top.shape[1]
    tile_tt = dot_high(top.T, top)
    tile_tb = dot_high(top.T, bottom)
    tile_bb = dot_high(bottom.T, bottom)
    gram = jnp.concatenate([jnp.concatenate([tile_tt, tile_tb], 1), jnp.concatenate([tile_tb.T, tile_bb], 1)], 0)
    basis = jacobi(gram, INNER_ROUNDS)
    moved = dot_high(jnp.concatenate([top, bottom], 1), basis)
    return moved[:, :half], moved[:, half:]


def reference(snapshots):
    total_rows = snapshots.shape[0]
    pairs = snapshots.shape[1] // (2 * BLOCK)
    grouped = jnp.transpose(snapshots.reshape(total_rows, pairs, 2, BLOCK), (1, 2, 0, 3))
    tops, bottoms = grouped[:, 0], grouped[:, 1]
    tops, bottoms = lax.map(pair_step, (tops, bottoms))
    new_tops = jnp.concatenate([tops[:1], bottoms[:1], tops[1:pairs - 1]], 0)
    new_bottoms = jnp.concatenate([bottoms[1:], tops[pairs - 1:]], 0)
    tops, bottoms = lax.map(pair_step, (new_tops, new_bottoms))
    stacked = jnp.stack([tops, bottoms], 1)
    return jnp.transpose(stacked, (2, 0, 1, 3)).reshape(total_rows, pairs * 2 * BLOCK)
```

```python
import functools

import jax
import jax.numpy as jnp
from jax import lax
from jax.experimental import pallas as pl
from jax.experimental.pallas import tpu as pltpu
from jax.sharding import PartitionSpec as P

INNER_ROUNDS = 10
HALF = 128
CHUNK = 256
MESH = pl.DeviceIdType.MESH
F32 = jnp.float32
BF16 = jnp.bfloat16


def split(value):
    high = value.astype(BF16)
    return high, (value - high.astype(F32)).astype(BF16)


def dot(left, right):
    return jnp.dot(left, right, preferred_element_type=F32)


def dot_rows(left, right):
    return lax.dot_general(left, right, (((0,), (0,)), ((), ())), preferred_element_type=F32)


def exact(left, right):
    return jnp.dot(left, right, precision=lax.Precision.HIGHEST, preferred_element_type=F32)


def iota(shape, axis):
    return lax.broadcasted_iota(jnp.int32, shape, axis)


def reversal():
    return (iota((HALF, HALF), 0) + iota((HALF, HALF), 1) == HALF - 1).astype(F32)


def shifted(first, second, axis):
    place = iota(first.shape, axis)
    mixed = jnp.where(place == 0, first, second)
    new_first = jnp.where(place == HALF - 1, second, pltpu.roll(first, HALF - 1, axis))
    new_second = jnp.where(place == 0, second, pltpu.roll(mixed, 1, axis))
    return new_first, new_second


def angles(diag_first, diag_second, cross, turn):
    slot = iota((1, HALF), 1)
    upper = jnp.where(slot == 0, 2 * HALF - 1, jnp.where(turn >= slot, turn - slot, turn - slot + 2 * HALF - 1))
    lead = turn + slot < upper
    gap = diag_first - diag_second
    gap_lead = jnp.where(lead, gap, -gap)
    height = jnp.where(gap_lead >= 0, -2.0, 2.0) * cross
    width = jnp.abs(gap)
    tall = jnp.abs(height)
    big = jnp.maximum(width, tall)
    safe = jnp.where(big > 0, big, 1.0)
    ratio = jnp.minimum(width, tall) / safe
    total = width + big * jnp.sqrt(1.0 + ratio * ratio)
    tangent = height / jnp.where(total > 0, total, 1.0)
    cosine = 1.0 / jnp.sqrt(1.0 + tangent * tangent)
    sine = tangent * cosine
    return cosine, jnp.where(lead, -sine, sine)


def solve(tt, tb, bb, work, basis):
    flip = reversal()
    tb = exact(tb, flip)
    work[0] = tt
    work[1] = tb
    work[2] = tb.T
    work[3] = exact(flip, exact(bb, flip))
    basis[0] = (iota((2 * HALF, HALF), 0) == iota((2 * HALF, HALF), 1)).astype(F32)
    basis[1] = (iota((2 * HALF, HALF), 0) + iota((2 * HALF, HALF), 1) == 2 * HALF - 1).astype(F32)

    def turn(index, carry):
        eye = iota((HALF, HALF), 0) == iota((HALF, HALF), 1)
        tt, tb, bt, bb = work[0], work[1], work[2], work[3]

        def diagonal(block):
            return jnp.sum(jnp.where(eye, block, 0.0), axis=0, keepdims=True)

        cosine, factor = angles(diagonal(tt), diagonal(bb), diagonal(tb), index)
        cosine_rows = jnp.broadcast_to(cosine, (HALF, HALF)).T
        factor_rows = jnp.broadcast_to(factor, (HALF, HALF)).T
        tt, tb = tt * cosine + tb * factor, tb * cosine - tt * factor
        bt, bb = bt * cosine + bb * factor, bb * cosine - bt * factor
        tt, bt = tt * cosine_rows + bt * factor_rows, bt * cosine_rows - tt * factor_rows
        tb, bb = tb * cosine_rows + bb * factor_rows, bb * cosine_rows - tb * factor_rows
        tt, tb = shifted(tt, tb, 1)
        bt, bb = shifted(bt, bb, 1)
        tt, bt = shifted(tt, bt, 0)
        tb, bb = shifted(tb, bb, 0)
        work[0], work[1], work[2], work[3] = tt, tb, bt, bb
        first, second = basis[0], basis[1]
        first, second = first * cosine + second * factor, second * cosine - first * factor
        basis[0], basis[1] = shifted(first, second, 1)
        return carry

    lax.fori_loop(0, INNER_ROUNDS, turn, 0)

    count = 2 * HALF - 1
    slot = iota((HALF, 2 * HALF), 0)
    natural = iota((HALF, 2 * HALF), 1)
    back = INNER_ROUNDS - slot
    place = jnp.where(slot == 0, count, jnp.where(back >= 0, back, back + count))
    first_place = natural == slot + INNER_ROUNDS
    second_place = natural == place

    high = []
    for part in zip(split(basis[0]), split(basis[1])):
        high.append((dot(part[0], first_place.astype(BF16)) + dot(part[1], second_place.astype(BF16))).astype(BF16))

    def turned():
        a, b = first_place.astype(F32), second_place.astype(F32)
        upper = exact(work[0], a) + exact(work[1], b)
        lower = exact(work[2], a) + exact(work[3], b)

        def block(columns):
            left = slice(columns * HALF, (columns + 1) * HALF)
            return exact(a[:, left].T, upper[:, left]) + exact(b[:, left].T, lower[:, left])

        return block(0), block(1)

    return high[0], high[1], turned


def times_basis(high, low, basis_high, basis_low):
    return dot(high, basis_high) + dot(low, basis_high) + dot(high, basis_low)


class Sum:
    def __init__(self, mine, parts, total, sems, n):
        self.mine, self.parts, self.total, self.sems, self.n = mine, parts, total, sems, n
        self.me = lax.axis_index("row")

    def each(self, action):
        def step(i, carry):
            peer = lax.rem(self.me + i, self.n)
            action(peer)
            return carry

        lax.fori_loop(1, self.n, step, 0)

    def drain(self, source, index):
        view = source.at[pl.ds(0, self.n - 1)]
        pltpu.make_async_copy(view, view, self.sems.at[index]).wait()

    def scatter(self):
        self.each(
            lambda peer: pltpu.make_async_remote_copy(
                src_ref=self.mine.at[peer],
                dst_ref=self.parts.at[self.me],
                send_sem=self.sems.at[0],
                recv_sem=self.sems.at[1],
                device_id={"row": peer},
                device_id_type=MESH,
            ).start()
        )
        self.parts[self.me] = self.mine[self.me]

    def add(self):
        self.drain(self.parts, 1)
        total = self.parts[0]
        for i in range(1, self.n):
            total = total + self.parts[i]
        return total

    def gather(self, piece):
        self.total[self.me] = piece
        self.each(
            lambda peer: pltpu.make_async_remote_copy(
                src_ref=self.total.at[self.me],
                dst_ref=self.total.at[self.me],
                send_sem=self.sems.at[2],
                recv_sem=self.sems.at[3],
                device_id={"row": peer},
                device_id_type=MESH,
            ).start()
        )
        self.drain(self.total, 3)

    def finish(self):
        self.drain(self.mine, 0)
        self.drain(self.total, 2)


def kernel(
    n, cycle, x_hbm, t2, b2, w_ref,
    x, xh, xl, left, right, gram,
    mine1, parts1, total1, mine2, parts2, total2,
    work, basis, blocks, got_blocks,
    load_sems, sums1, sums2, block_sems, chunk_sems,
):
    row, col = lax.axis_index("row"), lax.axis_index("col")
    rows = x.shape[0]
    chunks = rows // CHUNK
    is_head, is_tail = col == 0, col == cycle - 1

    def load(c):
        where = pl.ds(c * CHUNK, CHUNK)
        return pltpu.make_async_copy(x_hbm.at[where], x.at[where], load_sems.at[c])

    for c in range(chunks):
        load(c).start()

    barrier = pltpu.get_barrier_semaphore()

    def greet(i, carry):
        pl.semaphore_signal(barrier, inc=1, device_id={"row": lax.rem(row + i, n)}, device_id_type=MESH)
        return carry

    lax.fori_loop(1, n, greet, 0)

    @pl.when(jnp.logical_not(is_tail))
    def _():
        pl.semaphore_signal(barrier, inc=1, device_id={"col": col + 1}, device_id_type=MESH)

    @pl.when(jnp.logical_not(is_head))
    def _():
        pl.semaphore_signal(barrier, inc=1, device_id={"col": col - 1}, device_id_type=MESH)

    gram[...] = jnp.zeros_like(gram)
    for c in range(chunks):
        load(c).wait()
        where = pl.ds(c * CHUNK, CHUNK)
        high, low = split(x[where])
        xh[where] = high
        xl[where] = low
        gram[0] += dot_rows(high, high) + dot_rows(low, low)
        gram[1] += dot_rows(high, low)
    full = gram[0] + (gram[1] + gram[1].T)
    tt, tb, bb = full[:HALF, :HALF], full[:HALF, HALF:], full[HALF:, HALF:]
    below = iota((HALF, HALF), 0) >= iota((HALF, HALF), 1)
    eye = iota((HALF, HALF), 0) == iota((HALF, HALF), 1)
    folded = jnp.where(below, tt, bb)
    size1 = 2 * HALF // n
    mine1[:, :size1] = jnp.concatenate([tb, folded], 0).reshape(n, size1, HALF)
    corner = jnp.sum(jnp.where(eye, bb, 0.0), axis=0, keepdims=True)
    mine1[:, size1:] = jnp.broadcast_to(corner[None], (n, 1, HALF))

    inner = jnp.logical_not(jnp.logical_or(is_head, is_tail))

    @pl.when(inner)
    def _():
        pl.semaphore_wait(barrier, n + 1)

    @pl.when(jnp.logical_not(inner))
    def _():
        pl.semaphore_wait(barrier, n)

    sum1 = Sum(mine1, parts1, total1, sums1, n)
    sum1.scatter()
    piece = sum1.add()
    corner = piece[size1:]
    sum1.gather(piece[:size1])
    whole = total1[...].reshape(2 * HALF, HALF)
    tb, folded = whole[:HALF], whole[HALF:]
    turned_fold = folded.T
    tt = jnp.where(below, folded, turned_fold)
    bb = jnp.where(below, turned_fold, folded)
    bb = jnp.where(eye, jnp.broadcast_to(corner, (HALF, HALF)), bb)

    basis_high, basis_low, turned = solve(tt, tb, bb, work, basis)

    def send(kind, c):
        if c is None:
            source, target, sems = blocks.at[kind], got_blocks.at[kind], block_sems
            index = kind
        else:
            where = pl.ds(c * CHUNK, CHUNK)
            source = (right if kind == 0 else left).at[where]
            target = (t2 if kind == 0 else b2).at[where]
            sems = chunk_sems
            index = kind * chunks + c
        return pltpu.make_async_remote_copy(
            src_ref=source,
            dst_ref=target,
            send_sem=sems.at[0, index],
            recv_sem=sems.at[1, index],
            device_id={"col": col + 1 if kind == 0 else col - 1},
            device_id_type=MESH,
        )

    def start(c):
        @pl.when(jnp.logical_not(is_tail))
        def _():
            send(0, c).start()

        @pl.when(jnp.logical_not(is_head))
        def _():
            send(1, c).start()

    def arrive(c):
        @pl.when(jnp.logical_not(is_head))
        def _():
            send(0, c).wait_recv()

        @pl.when(jnp.logical_not(is_tail))
        def _():
            send(1, c).wait_recv()

    def left_device(c):
        @pl.when(jnp.logical_not(is_tail))
        def _():
            send(0, c).wait_send()

        @pl.when(jnp.logical_not(is_head))
        def _():
            send(1, c).wait_send()

    for c in range(chunks):
        where = pl.ds(c * CHUNK, CHUNK)
        moved = times_basis(xh[where], xl[where], basis_high, basis_low)
        top, bottom = moved[:, :HALF], moved[:, HALF:]
        right[where] = jnp.where(is_head, bottom, top)
        left[where] = bottom

        @pl.when(is_head)
        def _():
            t2[where] = top

        @pl.when(is_tail)
        def _():
            b2[where] = top

        start(c)

    tt, bb = turned()
    blocks[0] = jnp.where(is_head, bb, tt)
    blocks[1] = bb

    @pl.when(is_head)
    def _():
        got_blocks[0] = tt

    @pl.when(is_tail)
    def _():
        got_blocks[1] = tt

    start(None)
    gram[...] = jnp.zeros_like(gram)
    for c in range(chunks):
        arrive(c)
        where = pl.ds(c * CHUNK, CHUNK)
        th, tl = split(t2[where])
        bh, bl = split(b2[where])
        gram[0, :HALF, :HALF] += dot_rows(th, bh) + dot_rows(tl, bh) + dot_rows(th, bl)
    mine2[...] = gram[0, :HALF, :HALF].reshape(mine2.shape)
    sum2 = Sum(mine2, parts2, total2, sums2, n)
    sum2.scatter()
    sum2.gather(sum2.add())
    arrive(None)
    tb = total2[...].reshape(HALF, HALF)
    basis_high, basis_low, _ = solve(got_blocks[0], tb, got_blocks[1], work, basis)
    w_ref[0] = basis_high
    w_ref[1] = basis_low

    sum1.finish()
    sum2.finish()
    for c in range(chunks):
        left_device(c)
    left_device(None)


def last(t2, b2, w_ref, out):
    high, low = split(jnp.concatenate([t2[...], b2[...]], 1))
    out[...] = times_basis(high, low, w_ref[0], w_ref[1])


def local(n, cycle, snapshots):
    rows = snapshots.shape[0]
    chunks = rows // CHUNK
    dma = pltpu.SemaphoreType.DMA
    vmem = pl.BlockSpec(memory_space=pltpu.VMEM)
    size1, size2 = 2 * HALF // n, HALF // n
    t2, b2, w = pl.pallas_call(
        functools.partial(kernel, n, cycle),
        out_shape=[
            jax.ShapeDtypeStruct((rows, HALF), F32),
            jax.ShapeDtypeStruct((rows, HALF), F32),
            jax.ShapeDtypeStruct((2, 2 * HALF, 2 * HALF), BF16),
        ],
        in_specs=[pl.BlockSpec(memory_space=pl.ANY)],
        out_specs=[vmem] * 3,
        scratch_shapes=[
            pltpu.VMEM((rows, 2 * HALF), F32),
            pltpu.VMEM((rows, 2 * HALF), BF16),
            pltpu.VMEM((rows, 2 * HALF), BF16),
            pltpu.VMEM((rows, HALF), F32),
            pltpu.VMEM((rows, HALF), F32),
            pltpu.VMEM((2, 2 * HALF, 2 * HALF), F32),
            pltpu.VMEM((n, size1 + 1, HALF), F32),
            pltpu.VMEM((n, size1 + 1, HALF), F32),
            pltpu.VMEM((n, size1, HALF), F32),
            pltpu.VMEM((n, size2, HALF), F32),
            pltpu.VMEM((n, size2, HALF), F32),
            pltpu.VMEM((n, size2, HALF), F32),
            pltpu.VMEM((4, HALF, HALF), F32),
            pltpu.VMEM((2, 2 * HALF, HALF), F32),
            pltpu.VMEM((2, HALF, HALF), F32),
            pltpu.VMEM((2, HALF, HALF), F32),
            dma((chunks,)),
            dma((4,)),
            dma((4,)),
            dma((2, 2)),
            dma((2, 2 * chunks)),
        ],
        compiler_params=pltpu.CompilerParams(
            collective_id=0, has_side_effects=True, vmem_limit_bytes=40 << 20
        ),
    )(snapshots)
    return pl.pallas_call(
        last,
        grid=(rows // CHUNK,),
        out_shape=jax.ShapeDtypeStruct((rows, 2 * HALF), F32),
        in_specs=[
            pl.BlockSpec((CHUNK, HALF), lambda i: (i, 0)),
            pl.BlockSpec((CHUNK, HALF), lambda i: (i, 0)),
            pl.BlockSpec((2, 2 * HALF, 2 * HALF), lambda i: (0, 0, 0)),
        ],
        out_specs=pl.BlockSpec((CHUNK, 2 * HALF), lambda i: (i, 0)),
    )(t2, b2, w)


def solution(mesh):
    return jax.shard_map(
        functools.partial(local, mesh.shape["row"], mesh.shape["col"]),
        mesh=mesh,
        in_specs=(P("row", "col"),),
        out_specs=P("row", "col"),
        check_vma=False,
    )
```

```python
import functools

import jax
import jax.numpy as jnp
from jax import lax
from jax.experimental import pallas as pl
from jax.experimental.pallas import tpu as pltpu
from jax.sharding import PartitionSpec as P

INNER_ROUNDS = 10
HALF = 128
CHUNK = 256
MESH = pl.DeviceIdType.MESH
F32 = jnp.float32
BF16 = jnp.bfloat16


def split(value):
    high = value.astype(BF16)
    return high, (value - high.astype(F32)).astype(BF16)


def dot(left, right):
    return jnp.dot(left, right, preferred_element_type=F32)


def dot_rows(left, right):
    return lax.dot_general(left, right, (((0,), (0,)), ((), ())), preferred_element_type=F32)


def exact(left, right):
    return jnp.dot(left, right, precision=lax.Precision.HIGHEST, preferred_element_type=F32)


def iota(shape, axis):
    return lax.broadcasted_iota(jnp.int32, shape, axis)


def reversal():
    return (iota((HALF, HALF), 0) + iota((HALF, HALF), 1) == HALF - 1).astype(F32)


def shifted(first, second, axis):
    place = iota(first.shape, axis)
    mixed = jnp.where(place == 0, first, second)
    new_first = jnp.where(place == HALF - 1, second, pltpu.roll(first, HALF - 1, axis))
    new_second = jnp.where(place == 0, second, pltpu.roll(mixed, 1, axis))
    return new_first, new_second


def angles(diag_first, diag_second, cross, turn):
    slot = iota((1, HALF), 1)
    upper = jnp.where(slot == 0, 2 * HALF - 1, jnp.where(turn >= slot, turn - slot, turn - slot + 2 * HALF - 1))
    lead = turn + slot < upper
    gap = diag_first - diag_second
    gap_lead = jnp.where(lead, gap, -gap)
    height = jnp.where(gap_lead >= 0, -2.0, 2.0) * cross
    width = jnp.abs(gap)
    tall = jnp.abs(height)
    big = jnp.maximum(width, tall)
    safe = jnp.where(big > 0, big, 1.0)
    ratio = jnp.minimum(width, tall) / safe
    total = width + big * jnp.sqrt(1.0 + ratio * ratio)
    tangent = height / jnp.where(total > 0, total, 1.0)
    cosine = 1.0 / jnp.sqrt(1.0 + tangent * tangent)
    sine = tangent * cosine
    return cosine, jnp.where(lead, -sine, sine)


def solve(tt, tb, bb, work, basis):
    flip = reversal()
    tb = exact(tb, flip)
    work[0] = tt
    work[1] = tb
    work[2] = tb.T
    work[3] = exact(flip, exact(bb, flip))
    basis[0] = (iota((2 * HALF, HALF), 0) == iota((2 * HALF, HALF), 1)).astype(F32)
    basis[1] = (iota((2 * HALF, HALF), 0) + iota((2 * HALF, HALF), 1) == 2 * HALF - 1).astype(F32)

    def turn(index, carry):
        eye = iota((HALF, HALF), 0) == iota((HALF, HALF), 1)
        tt, tb, bt, bb = work[0], work[1], work[2], work[3]

        def diagonal(block):
            return jnp.sum(jnp.where(eye, block, 0.0), axis=0, keepdims=True)

        cosine, factor = angles(diagonal(tt), diagonal(bb), diagonal(tb), index)
        cosine_rows = jnp.broadcast_to(cosine, (HALF, HALF)).T
        factor_rows = jnp.broadcast_to(factor, (HALF, HALF)).T
        tt, tb = tt * cosine + tb * factor, tb * cosine - tt * factor
        bt, bb = bt * cosine + bb * factor, bb * cosine - bt * factor
        tt, bt = tt * cosine_rows + bt * factor_rows, bt * cosine_rows - tt * factor_rows
        tb, bb = tb * cosine_rows + bb * factor_rows, bb * cosine_rows - tb * factor_rows
        tt, tb = shifted(tt, tb, 1)
        bt, bb = shifted(bt, bb, 1)
        tt, bt = shifted(tt, bt, 0)
        tb, bb = shifted(tb, bb, 0)
        work[0], work[1], work[2], work[3] = tt, tb, bt, bb
        first, second = basis[0], basis[1]
        first, second = first * cosine + second * factor, second * cosine - first * factor
        basis[0], basis[1] = shifted(first, second, 1)
        return carry

    lax.fori_loop(0, INNER_ROUNDS, turn, 0)

    count = 2 * HALF - 1
    slot = iota((HALF, 2 * HALF), 0)
    natural = iota((HALF, 2 * HALF), 1)
    back = INNER_ROUNDS - slot
    place = jnp.where(slot == 0, count, jnp.where(back >= 0, back, back + count))
    first_place = natural == slot + INNER_ROUNDS
    second_place = natural == place

    high = []
    for part in zip(split(basis[0]), split(basis[1])):
        high.append((dot(part[0], first_place.astype(BF16)) + dot(part[1], second_place.astype(BF16))).astype(BF16))

    def turned():
        a, b = first_place.astype(F32), second_place.astype(F32)
        upper = exact(work[0], a) + exact(work[1], b)
        lower = exact(work[2], a) + exact(work[3], b)

        def block(columns):
            left = slice(columns * HALF, (columns + 1) * HALF)
            return exact(a[:, left].T, upper[:, left]) + exact(b[:, left].T, lower[:, left])

        return block(0), block(1)

    return high[0], high[1], turned


def times_basis(high, low, basis_high, basis_low):
    return dot(high, basis_high) + dot(low, basis_high) + dot(high, basis_low)


class Sum:
    def __init__(self, mine, parts, total, sems, n):
        self.mine, self.parts, self.total, self.sems, self.n = mine, parts, total, sems, n
        self.me = lax.axis_index("row")

    def each(self, action):
        half = self.n // 2
        group, place = self.me // half, lax.rem(self.me, half)

        def peer(k, other):
            offset = half // 2 + (1 - 2 * lax.rem(k, 2)) * ((k + 1) // 2)
            return lax.rem(group + other, 2) * half + lax.rem(place + offset, half)

        def step(k, carry):
            action(peer(k, 1))
            action(peer(k, 0))
            return carry

        lax.fori_loop(0, half - 1, step, 0)
        action(lax.rem(group + 1, 2) * half + place)

    def drain(self, source, index):
        view = source.at[pl.ds(0, self.n - 1)]
        pltpu.make_async_copy(view, view, self.sems.at[index]).wait()

    def scatter(self):
        self.each(
            lambda peer: pltpu.make_async_remote_copy(
                src_ref=self.mine.at[peer],
                dst_ref=self.parts.at[self.me],
                send_sem=self.sems.at[0],
                recv_sem=self.sems.at[1],
                device_id={"row": peer},
                device_id_type=MESH,
            ).start()
        )
        self.parts[self.me] = self.mine[self.me]

    def add(self):
        self.drain(self.parts, 1)
        total = self.parts[0]
        for i in range(1, self.n):
            total = total + self.parts[i]
        return total

    def gather(self, piece):
        self.total[self.me] = piece
        self.each(
            lambda peer: pltpu.make_async_remote_copy(
                src_ref=self.total.at[self.me],
                dst_ref=self.total.at[self.me],
                send_sem=self.sems.at[2],
                recv_sem=self.sems.at[3],
                device_id={"row": peer},
                device_id_type=MESH,
            ).start()
        )
        self.drain(self.total, 3)

    def finish(self):
        self.drain(self.mine, 0)
        self.drain(self.total, 2)


def kernel(
    n, cycle, x_hbm, t2, b2, w_ref,
    x, xh, xl, left, right, gram,
    mine1, parts1, total1, mine2, parts2, total2,
    work, basis, blocks, got_blocks,
    load_sems, sums1, sums2, block_sems, chunk_sems,
):
    row, col = lax.axis_index("row"), lax.axis_index("col")
    rows = x.shape[0]
    chunks = rows // CHUNK
    is_head, is_tail = col == 0, col == cycle - 1

    def load(c):
        where = pl.ds(c * CHUNK, CHUNK)
        return pltpu.make_async_copy(x_hbm.at[where], x.at[where], load_sems.at[c])

    for c in range(chunks):
        load(c).start()

    barrier = pltpu.get_barrier_semaphore()

    def greet(i, carry):
        pl.semaphore_signal(barrier, inc=1, device_id={"row": lax.rem(row + i, n)}, device_id_type=MESH)
        return carry

    lax.fori_loop(1, n, greet, 0)

    @pl.when(jnp.logical_not(is_tail))
    def _():
        pl.semaphore_signal(barrier, inc=1, device_id={"col": col + 1}, device_id_type=MESH)

    @pl.when(jnp.logical_not(is_head))
    def _():
        pl.semaphore_signal(barrier, inc=1, device_id={"col": col - 1}, device_id_type=MESH)

    gram[...] = jnp.zeros_like(gram)
    for c in range(chunks):
        load(c).wait()
        where = pl.ds(c * CHUNK, CHUNK)
        high, low = split(x[where])
        xh[where] = high
        xl[where] = low
        gram[0] += dot_rows(high, high) + dot_rows(low, low)
        gram[1] += dot_rows(high, low)
    full = gram[0] + (gram[1] + gram[1].T)
    tt, tb, bb = full[:HALF, :HALF], full[:HALF, HALF:], full[HALF:, HALF:]
    below = iota((HALF, HALF), 0) >= iota((HALF, HALF), 1)
    eye = iota((HALF, HALF), 0) == iota((HALF, HALF), 1)
    folded = jnp.where(below, tt, bb)
    size1 = 2 * HALF // n
    mine1[:, :size1] = jnp.concatenate([tb, folded], 0).reshape(n, size1, HALF)
    corner = jnp.sum(jnp.where(eye, bb, 0.0), axis=0, keepdims=True)
    mine1[:, size1:] = jnp.broadcast_to(corner[None], (n, 1, HALF))

    inner = jnp.logical_not(jnp.logical_or(is_head, is_tail))

    @pl.when(inner)
    def _():
        pl.semaphore_wait(barrier, n + 1)

    @pl.when(jnp.logical_not(inner))
    def _():
        pl.semaphore_wait(barrier, n)

    sum1 = Sum(mine1, parts1, total1, sums1, n)
    sum1.scatter()
    piece = sum1.add()
    corner = piece[size1:]
    sum1.gather(piece[:size1])
    whole = total1[...].reshape(2 * HALF, HALF)
    tb, folded = whole[:HALF], whole[HALF:]
    turned_fold = folded.T
    tt = jnp.where(below, folded, turned_fold)
    bb = jnp.where(below, turned_fold, folded)
    bb = jnp.where(eye, jnp.broadcast_to(corner, (HALF, HALF)), bb)

    basis_high, basis_low, turned = solve(tt, tb, bb, work, basis)

    def send(kind, c):
        if c is None:
            source, target, sems = blocks.at[kind], got_blocks.at[kind], block_sems
            index = kind
        else:
            where = pl.ds(c * CHUNK, CHUNK)
            source = (right if kind == 0 else left).at[where]
            target = (t2 if kind == 0 else b2).at[where]
            sems = chunk_sems
            index = kind * chunks + c
        return pltpu.make_async_remote_copy(
            src_ref=source,
            dst_ref=target,
            send_sem=sems.at[0, index],
            recv_sem=sems.at[1, index],
            device_id={"col": col + 1 if kind == 0 else col - 1},
            device_id_type=MESH,
        )

    def start(c):
        @pl.when(jnp.logical_not(is_tail))
        def _():
            send(0, c).start()

        @pl.when(jnp.logical_not(is_head))
        def _():
            send(1, c).start()

    def arrive(c):
        @pl.when(jnp.logical_not(is_head))
        def _():
            send(0, c).wait_recv()

        @pl.when(jnp.logical_not(is_tail))
        def _():
            send(1, c).wait_recv()

    def left_device(c):
        @pl.when(jnp.logical_not(is_tail))
        def _():
            send(0, c).wait_send()

        @pl.when(jnp.logical_not(is_head))
        def _():
            send(1, c).wait_send()

    for c in range(chunks):
        where = pl.ds(c * CHUNK, CHUNK)
        moved = times_basis(xh[where], xl[where], basis_high, basis_low)
        top, bottom = moved[:, :HALF], moved[:, HALF:]
        right[where] = jnp.where(is_head, bottom, top)
        left[where] = bottom

        @pl.when(is_head)
        def _():
            t2[where] = top

        @pl.when(is_tail)
        def _():
            b2[where] = top

        start(c)

    tt, bb = turned()
    blocks[0] = jnp.where(is_head, bb, tt)
    blocks[1] = bb

    @pl.when(is_head)
    def _():
        got_blocks[0] = tt

    @pl.when(is_tail)
    def _():
        got_blocks[1] = tt

    start(None)
    gram[...] = jnp.zeros_like(gram)
    for c in range(chunks):
        arrive(c)
        where = pl.ds(c * CHUNK, CHUNK)
        th, tl = split(t2[where])
        bh, bl = split(b2[where])
        gram[0, :HALF, :HALF] += dot_rows(th, bh) + dot_rows(tl, bh) + dot_rows(th, bl)
    mine2[...] = gram[0, :HALF, :HALF].reshape(mine2.shape)
    sum2 = Sum(mine2, parts2, total2, sums2, n)
    sum2.scatter()
    sum2.gather(sum2.add())
    arrive(None)
    tb = total2[...].reshape(HALF, HALF)
    basis_high, basis_low, _ = solve(got_blocks[0], tb, got_blocks[1], work, basis)
    w_ref[0] = basis_high
    w_ref[1] = basis_low

    sum1.finish()
    sum2.finish()
    for c in range(chunks):
        left_device(c)
    left_device(None)


def last(t2, b2, w_ref, out, held, sems):
    chunks = held.shape[0] // CHUNK

    def store(c):
        where = pl.ds(c * CHUNK, CHUNK)
        return pltpu.make_async_copy(held.at[where], out.at[where], sems.at[c])

    for c in range(chunks):
        where = pl.ds(c * CHUNK, CHUNK)
        high, low = split(jnp.concatenate([t2[where], b2[where]], 1))
        held[where] = times_basis(high, low, w_ref[0], w_ref[1])
        store(c).start()
    for c in range(chunks):
        store(c).wait()


def local(n, cycle, snapshots):
    rows = snapshots.shape[0]
    chunks = rows // CHUNK
    dma = pltpu.SemaphoreType.DMA
    vmem = pl.BlockSpec(memory_space=pltpu.VMEM)
    size1, size2 = 2 * HALF // n, HALF // n
    t2, b2, w = pl.pallas_call(
        functools.partial(kernel, n, cycle),
        out_shape=[
            jax.ShapeDtypeStruct((rows, HALF), F32),
            jax.ShapeDtypeStruct((rows, HALF), F32),
            jax.ShapeDtypeStruct((2, 2 * HALF, 2 * HALF), BF16),
        ],
        in_specs=[pl.BlockSpec(memory_space=pltpu.HBM)],
        out_specs=[vmem] * 3,
        scratch_shapes=[
            pltpu.VMEM((rows, 2 * HALF), F32),
            pltpu.VMEM((rows, 2 * HALF), BF16),
            pltpu.VMEM((rows, 2 * HALF), BF16),
            pltpu.VMEM((rows, HALF), F32),
            pltpu.VMEM((rows, HALF), F32),
            pltpu.VMEM((2, 2 * HALF, 2 * HALF), F32),
            pltpu.VMEM((n, size1 + 1, HALF), F32),
            pltpu.VMEM((n, size1 + 1, HALF), F32),
            pltpu.VMEM((n, size1, HALF), F32),
            pltpu.VMEM((n, size2, HALF), F32),
            pltpu.VMEM((n, size2, HALF), F32),
            pltpu.VMEM((n, size2, HALF), F32),
            pltpu.VMEM((4, HALF, HALF), F32),
            pltpu.VMEM((2, 2 * HALF, HALF), F32),
            pltpu.VMEM((2, HALF, HALF), F32),
            pltpu.VMEM((2, HALF, HALF), F32),
            dma((chunks,)),
            dma((4,)),
            dma((4,)),
            dma((2, 2)),
            dma((2, 2 * chunks)),
        ],
        compiler_params=pltpu.CompilerParams(
            collective_id=0, has_side_effects=True, vmem_limit_bytes=40 << 20
        ),
    )(pltpu.with_memory_space_constraint(snapshots, pltpu.HBM))
    return pl.pallas_call(
        last,
        out_shape=jax.ShapeDtypeStruct((rows, 2 * HALF), F32),
        in_specs=[vmem] * 3,
        out_specs=pl.BlockSpec(memory_space=pltpu.HBM),
        scratch_shapes=[pltpu.VMEM((rows, 2 * HALF), F32), dma((chunks,))],
        compiler_params=pltpu.CompilerParams(vmem_limit_bytes=24 << 20),
    )(t2, b2, w)


def solution(mesh):
    return jax.shard_map(
        functools.partial(local, mesh.shape["row"], mesh.shape["col"]),
        mesh=mesh,
        in_specs=(P("row", "col"),),
        out_specs=P("row", "col"),
        check_vma=False,
    )
```

```python
import functools

import jax
import jax.numpy as jnp
from jax import lax
from jax.experimental import pallas as pl
from jax.experimental.pallas import tpu as pltpu
from jax.sharding import PartitionSpec as P

INNER_ROUNDS = 10
HALF = 128
CHUNK = 256
EARLY = (1, 2)
SOLVE_ROWS = 64
MESH = pl.DeviceIdType.MESH
F32 = jnp.float32
BF16 = jnp.bfloat16


def split(value):
    high = value.astype(BF16)
    return high, (value - high.astype(F32)).astype(BF16)


def dot(left, right):
    return jnp.dot(left, right, preferred_element_type=F32)


def dot_rows(left, right):
    return lax.dot_general(left, right, (((0,), (0,)), ((), ())), preferred_element_type=F32)


def exact(left, right):
    return jnp.dot(left, right, precision=lax.Precision.HIGHEST, preferred_element_type=F32)


def exact_rows(left, right):
    return lax.dot_general(
        left, right, (((0,), (0,)), ((), ())), precision=lax.Precision.HIGHEST, preferred_element_type=F32
    )


def iota(shape, axis):
    return lax.broadcasted_iota(jnp.int32, shape, axis)


def reversal():
    return (iota((HALF, HALF), 0) + iota((HALF, HALF), 1) == HALF - 1).astype(F32)


def shifted(first, second, axis):
    place = iota(first.shape, axis)
    mixed = jnp.where(place == 0, first, second)
    new_first = jnp.where(place == HALF - 1, second, pltpu.roll(first, HALF - 1, axis))
    new_second = jnp.where(place == 0, second, pltpu.roll(mixed, 1, axis))
    return new_first, new_second


def angles(diag_first, diag_second, cross, turn):
    slot = iota((1, HALF), 1)
    upper = jnp.where(slot == 0, 2 * HALF - 1, jnp.where(turn >= slot, turn - slot, turn - slot + 2 * HALF - 1))
    lead = turn + slot < upper
    gap = diag_first - diag_second
    gap_lead = jnp.where(lead, gap, -gap)
    height = jnp.where(gap_lead >= 0, -2.0, 2.0) * cross
    width = jnp.abs(gap)
    big = jnp.maximum(width, jnp.abs(height))
    scale = 1.0 / jnp.where(big > 0, big, 1.0)
    width, height = width * scale, height * scale
    total = width + jnp.sqrt(width * width + height * height)
    tangent = height / jnp.where(big > 0, total, 1.0)
    cosine = lax.rsqrt(1.0 + tangent * tangent)
    sine = tangent * cosine
    return cosine, jnp.where(lead, -sine, sine)


def solve(tt, tb, bb, basis, image):
    basis[0] = (iota((2 * HALF, HALF), 0) == iota((2 * HALF, HALF), 1)).astype(F32)
    basis[1] = (iota((2 * HALF, HALF), 0) + iota((2 * HALF, HALF), 1) == 2 * HALF - 1).astype(F32)
    image[0] = jnp.concatenate([tt, tb.T], 0)
    image[1] = exact(jnp.concatenate([tb, bb], 0), reversal())

    def product(left, right):
        return jnp.sum((left * right).reshape(-1, 8, HALF), axis=0)

    def products(v_first, v_second, w_first, w_second):
        return product(v_first, w_first), product(v_second, w_second), product(v_first, w_second)

    def over_rows(sums):
        return tuple(jnp.sum(value, axis=0, keepdims=True) for value in sums)

    def turn(index, sums):
        cosine, factor = angles(*sums, index)
        found = None
        for c in range(2 * HALF // SOLVE_ROWS):
            where = pl.ds(c * SOLVE_ROWS, SOLVE_ROWS)
            fresh = []
            for ref in (basis, image):
                first, second = ref[0, where], ref[1, where]
                first, second = first * cosine + second * factor, second * cosine - first * factor
                first, second = shifted(first, second, 1)
                ref[0, where], ref[1, where] = first, second
                fresh += [first, second]
            part = products(*fresh)
            found = part if found is None else tuple(x + y for x, y in zip(found, part))
        return over_rows(found)

    sums = over_rows(products(basis[0], basis[1], image[0], image[1]))
    lax.fori_loop(0, INNER_ROUNDS, turn, sums)

    count = 2 * HALF - 1
    slot = iota((HALF, 2 * HALF), 0)
    natural = iota((HALF, 2 * HALF), 1)
    back = INNER_ROUNDS - slot
    place = jnp.where(slot == 0, count, jnp.where(back >= 0, back, back + count))
    first_place = natural == slot + INNER_ROUNDS
    second_place = natural == place

    high = []
    for part in zip(split(basis[0]), split(basis[1])):
        high.append((dot(part[0], first_place.astype(BF16)) + dot(part[1], second_place.astype(BF16))).astype(BF16))

    def turned():
        a, b = first_place.astype(F32), second_place.astype(F32)
        placed = exact(image[0], a) + exact(image[1], b)
        upper = exact_rows(basis[0], placed)
        lower = exact_rows(basis[1], placed)

        def block(columns):
            left = slice(columns * HALF, (columns + 1) * HALF)
            return exact(a[:, left].T, upper[:, left]) + exact(b[:, left].T, lower[:, left])

        return block(0), block(1)

    return high[0], high[1], turned


def times_basis(high, low, basis_high, basis_low):
    return dot(high, basis_high) + dot(low, basis_high) + dot(high, basis_low)


class Peers:
    def __init__(self, n):
        self.n, self.half = n, n // 2
        self.me = lax.axis_index("row")
        self.group, self.place = self.me // self.half, lax.rem(self.me, self.half)

    def at(self, other, offset):
        return lax.rem(self.group + other, 2) * self.half + lax.rem(self.place + self.half + offset, self.half)

    def each(self, action):
        def step(k, carry):
            offset = self.half // 2 + (1 - 2 * lax.rem(k, 2)) * ((k + 1) // 2)
            action(self.at(1, offset))
            action(self.at(0, offset))
            return carry

        lax.fori_loop(0, self.half - 1, step, 0)
        action(self.at(1, 0))

    def near(self, action):
        quarter = self.half // 4
        offsets = range(quarter - self.half // 2 + 1, quarter + 1)
        for offset in sorted(offsets, key=abs, reverse=True):
            action(self.at(1, offset))
            if offset:
                action(self.at(0, offset))


class Sum:
    def __init__(self, mine, parts, total, sems, peers, copies):
        self.mine, self.parts, self.total, self.sems, self.peers, self.copies = mine, parts, total, sems, peers, copies
        self.me = peers.me
        self.slices = peers.n // copies

    def slice_of(self, peer):
        if self.copies == 1:
            return peer
        half = self.peers.half
        return (peer // half) * (half // 2) + lax.rem(lax.rem(peer, half), half // 2)

    def drain(self, source, count, index):
        view = source.at[pl.ds(0, count)]
        pltpu.make_async_copy(view, view, self.sems.at[index]).wait()

    def scatter(self):
        self.peers.each(
            lambda peer: pltpu.make_async_remote_copy(
                src_ref=self.mine.at[self.slice_of(peer)],
                dst_ref=self.parts.at[self.me],
                send_sem=self.sems.at[0],
                recv_sem=self.sems.at[1],
                device_id={"row": peer},
                device_id_type=MESH,
            ).start()
        )
        self.parts[self.me] = self.mine[self.slice_of(self.me)]

    def add(self):
        self.drain(self.parts, self.peers.n - 1, 1)
        total = self.parts[0]
        for i in range(1, self.peers.n):
            total = total + self.parts[i]
        return total

    def gather(self, piece):
        own = self.slice_of(self.me)
        self.total[own] = piece
        (self.peers.each if self.copies == 1 else self.peers.near)(
            lambda peer: pltpu.make_async_remote_copy(
                src_ref=self.total.at[own],
                dst_ref=self.total.at[own],
                send_sem=self.sems.at[2],
                recv_sem=self.sems.at[3],
                device_id={"row": peer},
                device_id_type=MESH,
            ).start()
        )

    def wait(self):
        self.drain(self.total, self.slices - 1, 3)

    def finish(self):
        self.drain(self.parts, self.peers.n - 1, 0)
        self.drain(self.total, self.slices - 1, 2)


def kernel(
    n, cycle, x_hbm, t2, b2, w_ref,
    x, xh, xl, left, right, gram, got_rows, bases, got_bases,
    mine1, parts1, total1, mine2, parts2, total2,
    basis, image, blocks, got_blocks,
    load_sems, sums1, sums2, block_sems, base_sems, chunk_sems,
):
    col = lax.axis_index("col")
    chunks = x.shape[0] // CHUNK
    is_head, is_tail = col == 0, col == cycle - 1

    def load(c):
        where = pl.ds(c * CHUNK, CHUNK)
        return pltpu.make_async_copy(x_hbm.at[where], x.at[where], load_sems.at[c])

    for c in range(chunks):
        load(c).start()

    barrier = pltpu.get_barrier_semaphore()

    peers = Peers(n)
    peers.each(lambda peer: pl.semaphore_signal(barrier, inc=1, device_id={"row": peer}, device_id_type=MESH))

    @pl.when(jnp.logical_not(is_tail))
    def _():
        pl.semaphore_signal(barrier, inc=1, device_id={"col": col + 1}, device_id_type=MESH)

    @pl.when(jnp.logical_not(is_head))
    def _():
        pl.semaphore_signal(barrier, inc=1, device_id={"col": col - 1}, device_id_type=MESH)

    gram[...] = jnp.zeros_like(gram)
    for c in range(chunks):
        load(c).wait()
        where = pl.ds(c * CHUNK, CHUNK)
        high, low = split(x[where])
        xh[where] = high
        xl[where] = low
        gram[0] += dot_rows(high, high) + dot_rows(low, low)
        gram[1] += dot_rows(high, low)
    full = gram[0] + (gram[1] + gram[1].T)
    tt, tb, bb = full[:HALF, :HALF], full[:HALF, HALF:], full[HALF:, HALF:]
    below = iota((HALF, HALF), 0) >= iota((HALF, HALF), 1)
    eye = iota((HALF, HALF), 0) == iota((HALF, HALF), 1)
    folded = jnp.where(below, tt, bb)
    size1 = 2 * HALF // n
    mine1[:, :size1] = jnp.concatenate([tb, folded], 0).reshape(n, size1, HALF)
    corner = jnp.sum(jnp.where(eye, bb, 0.0), axis=0, keepdims=True)
    mine1[:, size1:] = jnp.broadcast_to(corner[None], (n, 1, HALF))

    inner = jnp.logical_not(jnp.logical_or(is_head, is_tail))

    @pl.when(inner)
    def _():
        pl.semaphore_wait(barrier, n + 1)

    @pl.when(jnp.logical_not(inner))
    def _():
        pl.semaphore_wait(barrier, n)

    def transfer(kind, source, target, sems, index):
        return pltpu.make_async_remote_copy(
            src_ref=source,
            dst_ref=target,
            send_sem=sems.at[0, index],
            recv_sem=sems.at[1, index],
            device_id={"col": col + 1 if kind == 0 else col - 1},
            device_id_type=MESH,
        )

    early = sum(EARLY)

    def rows_move(kind, c):
        where = pl.ds(c * CHUNK, CHUNK)
        if c < early:
            source, target = x.at[where], got_rows.at[kind, where]
        else:
            source, target = (left if kind else right).at[where], (b2 if kind else t2).at[where]
        return transfer(kind, source, target, chunk_sems, kind * chunks + c)

    def block_move(kind):
        return transfer(kind, blocks.at[kind], got_blocks.at[kind], block_sems, kind)

    def base_move(kind):
        return transfer(kind, bases.at[kind], got_bases.at[kind], base_sems, kind)

    def start(move):
        @pl.when(jnp.logical_not(is_tail))
        def _():
            move(0).start()

        @pl.when(jnp.logical_not(is_head))
        def _():
            move(1).start()

    def arrive(move):
        @pl.when(jnp.logical_not(is_head))
        def _():
            move(0).wait_recv()

        @pl.when(jnp.logical_not(is_tail))
        def _():
            move(1).wait_recv()

    def sent(move):
        @pl.when(jnp.logical_not(is_tail))
        def _():
            move(0).wait_send()

        @pl.when(jnp.logical_not(is_head))
        def _():
            move(1).wait_send()

    def rows(c):
        return lambda kind: rows_move(kind, c)

    sum1 = Sum(mine1, parts1, total1, sums1, peers, 1)
    sum1.scatter()
    for c in range(EARLY[0]):
        start(rows(c))
    piece = sum1.add()
    corner = piece[size1:]
    sum1.gather(piece[:size1])
    for c in range(EARLY[0], early):
        start(rows(c))

    @pl.when(is_head)
    def _():
        got_rows[0] = x[: early * CHUNK]

    @pl.when(is_tail)
    def _():
        got_rows[1] = x[: early * CHUNK]

    sum1.wait()
    whole = total1[...].reshape(2 * HALF, HALF)
    tb, folded = whole[:HALF], whole[HALF:]
    turned_fold = folded.T
    tt = jnp.where(below, folded, turned_fold)
    bb = jnp.where(below, turned_fold, folded)
    bb = jnp.where(eye, jnp.broadcast_to(corner, (HALF, HALF)), bb)

    basis_high, basis_low, turned = solve(tt, tb, bb, basis, image)

    whole_basis = basis_high.astype(F32) + basis_low.astype(F32)
    basis_top, basis_bottom = whole_basis[:, :HALF], whole_basis[:, HALF:]
    bases[0] = jnp.where(is_head, basis_bottom, basis_top)
    bases[1] = basis_bottom
    start(base_move)

    @pl.when(is_head)
    def _():
        got_bases[0] = basis_top

    @pl.when(is_tail)
    def _():
        got_bases[1] = basis_top

    for c in range(early, chunks):
        where = pl.ds(c * CHUNK, CHUNK)
        moved = times_basis(xh[where], xl[where], basis_high, basis_low)
        top, bottom = moved[:, :HALF], moved[:, HALF:]
        right[where] = jnp.where(is_head, bottom, top)
        left[where] = bottom

        @pl.when(is_head)
        def _():
            t2[where] = top

        @pl.when(is_tail)
        def _():
            b2[where] = top

        start(rows(c))

    tt, bb = turned()
    blocks[0] = jnp.where(is_head, bb, tt)
    blocks[1] = bb

    @pl.when(is_head)
    def _():
        got_blocks[0] = tt

    @pl.when(is_tail)
    def _():
        got_blocks[1] = tt

    start(block_move)

    for c in range(early):
        arrive(rows(c))
    arrive(base_move)
    got_top, got_bottom = split(got_bases[0]), split(got_bases[1])
    cross = jnp.zeros((HALF, HALF), F32)
    for c in range(chunks):
        where = pl.ds(c * CHUNK, CHUNK)
        if c < early:
            t2[where] = times_basis(*split(got_rows[0, where]), *got_top)
            b2[where] = times_basis(*split(got_rows[1, where]), *got_bottom)
        else:
            arrive(rows(c))
        th, tl = split(t2[where])
        bh, bl = split(b2[where])
        cross += dot_rows(th, bh) + dot_rows(tl, bh) + dot_rows(th, bl)
    mine2[...] = cross.reshape(mine2.shape)
    sum2 = Sum(mine2, parts2, total2, sums2, peers, 2)
    sum2.scatter()
    sum2.gather(sum2.add())
    arrive(block_move)
    sum2.wait()
    tb = total2[...].reshape(HALF, HALF)
    basis_high, basis_low, _ = solve(got_blocks[0], tb, got_blocks[1], basis, image)
    w_ref[0] = basis_high
    w_ref[1] = basis_low

    sum1.finish()
    sum2.finish()
    for c in range(chunks):
        sent(rows(c))
    sent(block_move)
    sent(base_move)


def last(t2, b2, w_ref, out, held, sems):
    chunks = held.shape[0] // CHUNK

    def store(c):
        where = pl.ds(c * CHUNK, CHUNK)
        return pltpu.make_async_copy(held.at[where], out.at[where], sems.at[c])

    for c in range(chunks):
        where = pl.ds(c * CHUNK, CHUNK)
        high, low = split(jnp.concatenate([t2[where], b2[where]], 1))
        held[where] = times_basis(high, low, w_ref[0], w_ref[1])
        store(c).start()
    for c in range(chunks):
        store(c).wait()


def local(n, cycle, snapshots):
    rows = snapshots.shape[0]
    chunks = rows // CHUNK
    dma = pltpu.SemaphoreType.DMA
    vmem = pl.BlockSpec(memory_space=pltpu.VMEM)
    size1, size2 = 2 * HALF // n, 2 * HALF // n
    t2, b2, w = pl.pallas_call(
        functools.partial(kernel, n, cycle),
        out_shape=[
            jax.ShapeDtypeStruct((rows, HALF), F32),
            jax.ShapeDtypeStruct((rows, HALF), F32),
            jax.ShapeDtypeStruct((2, 2 * HALF, 2 * HALF), BF16),
        ],
        in_specs=[pl.BlockSpec(memory_space=pltpu.HBM)],
        out_specs=[vmem] * 3,
        scratch_shapes=[
            pltpu.VMEM((rows, 2 * HALF), F32),
            pltpu.VMEM((rows, 2 * HALF), BF16),
            pltpu.VMEM((rows, 2 * HALF), BF16),
            pltpu.VMEM((rows, HALF), F32),
            pltpu.VMEM((rows, HALF), F32),
            pltpu.VMEM((2, 2 * HALF, 2 * HALF), F32),
            pltpu.VMEM((2, sum(EARLY) * CHUNK, 2 * HALF), F32),
            pltpu.VMEM((2, 2 * HALF, HALF), F32),
            pltpu.VMEM((2, 2 * HALF, HALF), F32),
            pltpu.VMEM((n, size1 + 1, HALF), F32),
            pltpu.VMEM((n, size1 + 1, HALF), F32),
            pltpu.VMEM((n, size1, HALF), F32),
            pltpu.VMEM((n // 2, size2, HALF), F32),
            pltpu.VMEM((n, size2, HALF), F32),
            pltpu.VMEM((n // 2, size2, HALF), F32),
            pltpu.VMEM((2, 2 * HALF, HALF), F32),
            pltpu.VMEM((2, 2 * HALF, HALF), F32),
            pltpu.VMEM((2, HALF, HALF), F32),
            pltpu.VMEM((2, HALF, HALF), F32),
            dma((chunks,)),
            dma((4,)),
            dma((4,)),
            dma((2, 2)),
            dma((2, 2)),
            dma((2, 2 * chunks)),
        ],
        compiler_params=pltpu.CompilerParams(
            collective_id=0, has_side_effects=True, vmem_limit_bytes=40 << 20
        ),
    )(pltpu.with_memory_space_constraint(snapshots, pltpu.HBM))
    return pl.pallas_call(
        last,
        out_shape=jax.ShapeDtypeStruct((rows, 2 * HALF), F32),
        in_specs=[vmem] * 3,
        out_specs=pl.BlockSpec(memory_space=pltpu.HBM),
        scratch_shapes=[pltpu.VMEM((rows, 2 * HALF), F32), dma((chunks,))],
        compiler_params=pltpu.CompilerParams(vmem_limit_bytes=24 << 20),
    )(t2, b2, w)


def solution(mesh):
    return jax.shard_map(
        functools.partial(local, mesh.shape["row"], mesh.shape["col"]),
        mesh=mesh,
        in_specs=(P("row", "col"),),
        out_specs=P("row", "col"),
        check_vma=False,
    )
```

```python
import functools

import jax
import jax.numpy as jnp
from jax import lax
from jax.experimental import pallas as pl
from jax.experimental.pallas import tpu as pltpu
from jax.sharding import PartitionSpec as P

INNER_ROUNDS = 10
HALF = 128
CHUNK = 256
EARLY = (1, 2)
SOLVE_ROWS = 64
MESH = pl.DeviceIdType.MESH
F32 = jnp.float32
BF16 = jnp.bfloat16


def split(value):
    high = value.astype(BF16)
    return high, (value - high.astype(F32)).astype(BF16)


def dot(left, right):
    return jnp.dot(left, right, preferred_element_type=F32)


def dot_rows(left, right):
    return lax.dot_general(left, right, (((0,), (0,)), ((), ())), preferred_element_type=F32)


def exact(left, right):
    return jnp.dot(left, right, precision=lax.Precision.HIGHEST, preferred_element_type=F32)


def exact_rows(left, right):
    return lax.dot_general(
        left, right, (((0,), (0,)), ((), ())), precision=lax.Precision.HIGHEST, preferred_element_type=F32
    )


def iota(shape, axis):
    return lax.broadcasted_iota(jnp.int32, shape, axis)


def reversal():
    return (iota((HALF, HALF), 0) + iota((HALF, HALF), 1) == HALF - 1).astype(F32)


def shifted(first, second, axis):
    place = iota(first.shape, axis)
    mixed = jnp.where(place == 0, first, second)
    new_first = jnp.where(place == HALF - 1, second, pltpu.roll(first, HALF - 1, axis))
    new_second = jnp.where(place == 0, second, pltpu.roll(mixed, 1, axis))
    return new_first, new_second


def angles(diag_first, diag_second, cross, turn):
    slot = iota((1, HALF), 1)
    upper = jnp.where(slot == 0, 2 * HALF - 1, jnp.where(turn >= slot, turn - slot, turn - slot + 2 * HALF - 1))
    lead = turn + slot < upper
    gap = diag_first - diag_second
    gap_lead = jnp.where(lead, gap, -gap)
    height = jnp.where(gap_lead >= 0, -2.0, 2.0) * cross
    width = jnp.abs(gap)
    big = jnp.maximum(width, jnp.abs(height))
    scale = 1.0 / jnp.where(big > 0, big, 1.0)
    width, height = width * scale, height * scale
    total = width + jnp.sqrt(width * width + height * height)
    tangent = height / jnp.where(big > 0, total, 1.0)
    cosine = lax.rsqrt(1.0 + tangent * tangent)
    sine = tangent * cosine
    return cosine, jnp.where(lead, -sine, sine)


def fresh_basis(basis):
    basis[0] = (iota((2 * HALF, HALF), 0) == iota((2 * HALF, HALF), 1)).astype(F32)
    basis[1] = (iota((2 * HALF, HALF), 0) + iota((2 * HALF, HALF), 1) == 2 * HALF - 1).astype(F32)


def turn_columns(ref, where, cosine, factor):
    first, second = ref[0, where], ref[1, where]
    first, second = first * cosine + second * factor, second * cosine - first * factor
    first, second = shifted(first, second, 1)
    ref[0, where], ref[1, where] = first, second
    return first, second


def places():
    count = 2 * HALF - 1
    slot = iota((HALF, 2 * HALF), 0)
    natural = iota((HALF, 2 * HALF), 1)
    back = INNER_ROUNDS - slot
    place = jnp.where(slot == 0, count, jnp.where(back >= 0, back, back + count))
    return natural == slot + INNER_ROUNDS, natural == place


def natural_basis(basis):
    first_place, second_place = places()
    a, b = first_place.astype(BF16), second_place.astype(BF16)
    return tuple((dot(x, a) + dot(y, b)).astype(BF16) for x, y in zip(split(basis[0]), split(basis[1])))


def rebuild(turns, basis):
    fresh_basis(basis)

    def turn(index, carry):
        cosine, factor = turns[0, pl.ds(index, 1)], turns[1, pl.ds(index, 1)]
        for c in range(2 * HALF // SOLVE_ROWS):
            turn_columns(basis, pl.ds(c * SOLVE_ROWS, SOLVE_ROWS), cosine, factor)
        return carry

    lax.fori_loop(0, INNER_ROUNDS, turn, 0)
    return natural_basis(basis)


def solve(tt, tb, bb, basis, image, turns=None):
    fresh_basis(basis)
    image[0] = jnp.concatenate([tt, tb.T], 0)
    image[1] = exact(jnp.concatenate([tb, bb], 0), reversal())

    def product(left, right):
        return jnp.sum((left * right).reshape(-1, 8, HALF), axis=0)

    def products(v_first, v_second, w_first, w_second):
        return product(v_first, w_first), product(v_second, w_second), product(v_first, w_second)

    def over_rows(sums):
        return tuple(jnp.sum(value, axis=0, keepdims=True) for value in sums)

    def turn(index, sums):
        cosine, factor = angles(*sums, index)
        if turns is not None:
            turns[0, pl.ds(index, 1)] = cosine
            turns[1, pl.ds(index, 1)] = factor
        found = None
        for c in range(2 * HALF // SOLVE_ROWS):
            where = pl.ds(c * SOLVE_ROWS, SOLVE_ROWS)
            part = products(*turn_columns(basis, where, cosine, factor), *turn_columns(image, where, cosine, factor))
            found = part if found is None else tuple(x + y for x, y in zip(found, part))
        return over_rows(found)

    sums = over_rows(products(basis[0], basis[1], image[0], image[1]))
    lax.fori_loop(0, INNER_ROUNDS, turn, sums)
    high, low = natural_basis(basis)

    def turned():
        a, b = (place.astype(F32) for place in places())
        placed = exact(image[0], a) + exact(image[1], b)
        upper = exact_rows(basis[0], placed)
        lower = exact_rows(basis[1], placed)

        def block(columns):
            left = slice(columns * HALF, (columns + 1) * HALF)
            return exact(a[:, left].T, upper[:, left]) + exact(b[:, left].T, lower[:, left])

        return block(0), block(1)

    return high, low, turned


def times_basis(high, low, basis_high, basis_low):
    return dot(high, basis_high) + dot(low, basis_high) + dot(high, basis_low)


class Peers:
    def __init__(self, n):
        self.n, self.half = n, n // 2
        self.me = lax.axis_index("row")
        self.group, self.place = self.me // self.half, lax.rem(self.me, self.half)

    def at(self, other, offset):
        return lax.rem(self.group + other, 2) * self.half + lax.rem(self.place + self.half + offset, self.half)

    def each(self, action):
        def step(k, carry):
            offset = self.half // 2 + (1 - 2 * lax.rem(k, 2)) * ((k + 1) // 2)
            action(self.at(1, offset))
            action(self.at(0, offset))
            return carry

        lax.fori_loop(0, self.half - 1, step, 0)
        action(self.at(1, 0))

    def near(self, action):
        quarter = self.half // 4
        offsets = range(quarter - self.half // 2 + 1, quarter + 1)
        for offset in sorted(offsets, key=abs, reverse=True):
            action(self.at(1, offset))
            if offset:
                action(self.at(0, offset))


class Sum:
    def __init__(self, mine, parts, total, sems, peers, copies):
        self.mine, self.parts, self.total, self.sems, self.peers, self.copies = mine, parts, total, sems, peers, copies
        self.me = peers.me
        self.slices = peers.n // copies

    def slice_of(self, peer):
        if self.copies == 1:
            return peer
        half = self.peers.half
        return (peer // half) * (half // 2) + lax.rem(lax.rem(peer, half), half // 2)

    def drain(self, source, count, index):
        view = source.at[pl.ds(0, count)]
        pltpu.make_async_copy(view, view, self.sems.at[index]).wait()

    def scatter(self):
        self.peers.each(
            lambda peer: pltpu.make_async_remote_copy(
                src_ref=self.mine.at[self.slice_of(peer)],
                dst_ref=self.parts.at[self.me],
                send_sem=self.sems.at[0],
                recv_sem=self.sems.at[1],
                device_id={"row": peer},
                device_id_type=MESH,
            ).start()
        )
        self.parts[self.me] = self.mine[self.slice_of(self.me)]

    def add(self):
        self.drain(self.parts, self.peers.n - 1, 1)
        total = self.parts[0]
        for i in range(1, self.peers.n):
            total = total + self.parts[i]
        return total

    def gather(self, piece):
        own = self.slice_of(self.me)
        self.total[own] = piece
        (self.peers.each if self.copies == 1 else self.peers.near)(
            lambda peer: pltpu.make_async_remote_copy(
                src_ref=self.total.at[own],
                dst_ref=self.total.at[own],
                send_sem=self.sems.at[2],
                recv_sem=self.sems.at[3],
                device_id={"row": peer},
                device_id_type=MESH,
            ).start()
        )

    def wait(self):
        self.drain(self.total, self.slices - 1, 3)

    def finish(self):
        self.drain(self.parts, self.peers.n - 1, 0)
        self.drain(self.total, self.slices - 1, 2)


def kernel(
    n, cycle, x_hbm, t2, b2, w_ref,
    x, xh, xl, left, right, gram, got_rows, turns, got_turns, other,
    mine1, parts1, total1, mine2, parts2, total2,
    basis, image, blocks, got_blocks,
    load_sems, sums1, sums2, block_sems, turn_sems, chunk_sems,
):
    col = lax.axis_index("col")
    chunks = x.shape[0] // CHUNK
    is_head, is_tail = col == 0, col == cycle - 1

    def load(c):
        where = pl.ds(c * CHUNK, CHUNK)
        return pltpu.make_async_copy(x_hbm.at[where], x.at[where], load_sems.at[c])

    for c in range(chunks):
        load(c).start()

    barrier = pltpu.get_barrier_semaphore()

    peers = Peers(n)
    peers.each(lambda peer: pl.semaphore_signal(barrier, inc=1, device_id={"row": peer}, device_id_type=MESH))

    @pl.when(jnp.logical_not(is_tail))
    def _():
        pl.semaphore_signal(barrier, inc=1, device_id={"col": col + 1}, device_id_type=MESH)

    @pl.when(jnp.logical_not(is_head))
    def _():
        pl.semaphore_signal(barrier, inc=1, device_id={"col": col - 1}, device_id_type=MESH)

    gram[...] = jnp.zeros_like(gram)
    for c in range(chunks):
        load(c).wait()
        where = pl.ds(c * CHUNK, CHUNK)
        high, low = split(x[where])
        xh[where] = high
        xl[where] = low
        gram[0] += dot_rows(high, high) + dot_rows(low, low)
        gram[1] += dot_rows(high, low)
    full = gram[0] + (gram[1] + gram[1].T)
    tt, tb, bb = full[:HALF, :HALF], full[:HALF, HALF:], full[HALF:, HALF:]
    below = iota((HALF, HALF), 0) >= iota((HALF, HALF), 1)
    eye = iota((HALF, HALF), 0) == iota((HALF, HALF), 1)
    folded = jnp.where(below, tt, bb)
    size1 = 2 * HALF // n
    mine1[:, :size1] = jnp.concatenate([tb, folded], 0).reshape(n, size1, HALF)
    corner = jnp.sum(jnp.where(eye, bb, 0.0), axis=0, keepdims=True)
    mine1[:, size1:] = jnp.broadcast_to(corner[None], (n, 1, HALF))

    inner = jnp.logical_not(jnp.logical_or(is_head, is_tail))

    @pl.when(inner)
    def _():
        pl.semaphore_wait(barrier, n + 1)

    @pl.when(jnp.logical_not(inner))
    def _():
        pl.semaphore_wait(barrier, n)

    def transfer(kind, source, target, sems, index):
        return pltpu.make_async_remote_copy(
            src_ref=source,
            dst_ref=target,
            send_sem=sems.at[0, index],
            recv_sem=sems.at[1, index],
            device_id={"col": col + 1 if kind == 0 else col - 1},
            device_id_type=MESH,
        )

    early = sum(EARLY)

    def rows_move(kind, c):
        where = pl.ds(c * CHUNK, CHUNK)
        if c < early:
            source, target = x.at[where], got_rows.at[kind, where]
        else:
            source, target = (left if kind else right).at[where], (b2 if kind else t2).at[where]
        return transfer(kind, source, target, chunk_sems, kind * chunks + c)

    def block_move(kind):
        return transfer(kind, blocks.at[kind], got_blocks.at[kind], block_sems, kind)

    def turn_move(kind):
        return transfer(kind, turns, got_turns.at[kind], turn_sems, kind)

    def start(move):
        @pl.when(jnp.logical_not(is_tail))
        def _():
            move(0).start()

        @pl.when(jnp.logical_not(is_head))
        def _():
            move(1).start()

    def arrive(move):
        @pl.when(jnp.logical_not(is_head))
        def _():
            move(0).wait_recv()

        @pl.when(jnp.logical_not(is_tail))
        def _():
            move(1).wait_recv()

    def sent(move):
        @pl.when(jnp.logical_not(is_tail))
        def _():
            move(0).wait_send()

        @pl.when(jnp.logical_not(is_head))
        def _():
            move(1).wait_send()

    def rows(c):
        return lambda kind: rows_move(kind, c)

    sum1 = Sum(mine1, parts1, total1, sums1, peers, 1)
    sum1.scatter()
    for c in range(EARLY[0]):
        start(rows(c))
    piece = sum1.add()
    corner = piece[size1:]
    sum1.gather(piece[:size1])
    for c in range(EARLY[0], early):
        start(rows(c))

    @pl.when(is_head)
    def _():
        got_rows[0] = x[: early * CHUNK]

    @pl.when(is_tail)
    def _():
        got_rows[1] = x[: early * CHUNK]

    sum1.wait()
    whole = total1[...].reshape(2 * HALF, HALF)
    tb, folded = whole[:HALF], whole[HALF:]
    turned_fold = folded.T
    tt = jnp.where(below, folded, turned_fold)
    bb = jnp.where(below, turned_fold, folded)
    bb = jnp.where(eye, jnp.broadcast_to(corner, (HALF, HALF)), bb)

    turns[...] = jnp.zeros_like(turns)
    basis_high, basis_low, turned = solve(tt, tb, bb, basis, image, turns)

    start(turn_move)

    @pl.when(is_head)
    def _():
        got_turns[0] = turns[...]

    @pl.when(is_tail)
    def _():
        got_turns[1] = turns[...]

    for c in range(early, chunks):
        where = pl.ds(c * CHUNK, CHUNK)
        moved = times_basis(xh[where], xl[where], basis_high, basis_low)
        top, bottom = moved[:, :HALF], moved[:, HALF:]
        right[where] = jnp.where(is_head, bottom, top)
        left[where] = bottom

        @pl.when(is_head)
        def _():
            t2[where] = top

        @pl.when(is_tail)
        def _():
            b2[where] = top

        start(rows(c))

    tt, bb = turned()
    blocks[0] = jnp.where(is_head, bb, tt)
    blocks[1] = bb

    @pl.when(is_head)
    def _():
        got_blocks[0] = tt

    @pl.when(is_tail)
    def _():
        got_blocks[1] = tt

    start(block_move)

    arrive(turn_move)
    got_top = [
        jnp.where(col == 1, part[:, HALF:], part[:, :HALF]) for part in rebuild(got_turns.at[0], other)
    ]
    got_bottom = [
        jnp.where(is_tail, part[:, :HALF], part[:, HALF:]) for part in rebuild(got_turns.at[1], other)
    ]
    for c in range(early):
        arrive(rows(c))
    cross = jnp.zeros((HALF, HALF), F32)
    for c in range(chunks):
        where = pl.ds(c * CHUNK, CHUNK)
        if c < early:
            t2[where] = times_basis(*split(got_rows[0, where]), *got_top)
            b2[where] = times_basis(*split(got_rows[1, where]), *got_bottom)
        else:
            arrive(rows(c))
        th, tl = split(t2[where])
        bh, bl = split(b2[where])
        cross += dot_rows(th, bh) + dot_rows(tl, bh) + dot_rows(th, bl)
    mine2[...] = cross.reshape(mine2.shape)
    sum2 = Sum(mine2, parts2, total2, sums2, peers, 2)
    sum2.scatter()
    sum2.gather(sum2.add())
    arrive(block_move)
    sum2.wait()
    tb = total2[...].reshape(HALF, HALF)
    basis_high, basis_low, _ = solve(got_blocks[0], tb, got_blocks[1], basis, image)
    w_ref[0] = basis_high
    w_ref[1] = basis_low

    sum1.finish()
    sum2.finish()
    for c in range(chunks):
        sent(rows(c))
    sent(block_move)
    sent(turn_move)


def last(t2, b2, w_ref, out, held, sems):
    chunks = held.shape[0] // CHUNK

    def store(c):
        where = pl.ds(c * CHUNK, CHUNK)
        return pltpu.make_async_copy(held.at[where], out.at[where], sems.at[c])

    for c in range(chunks):
        where = pl.ds(c * CHUNK, CHUNK)
        high, low = split(jnp.concatenate([t2[where], b2[where]], 1))
        held[where] = times_basis(high, low, w_ref[0], w_ref[1])
        store(c).start()
    for c in range(chunks):
        store(c).wait()


def local(n, cycle, snapshots):
    rows = snapshots.shape[0]
    chunks = rows // CHUNK
    dma = pltpu.SemaphoreType.DMA
    vmem = pl.BlockSpec(memory_space=pltpu.VMEM)
    size1, size2 = 2 * HALF // n, 2 * HALF // n
    t2, b2, w = pl.pallas_call(
        functools.partial(kernel, n, cycle),
        out_shape=[
            jax.ShapeDtypeStruct((rows, HALF), F32),
            jax.ShapeDtypeStruct((rows, HALF), F32),
            jax.ShapeDtypeStruct((2, 2 * HALF, 2 * HALF), BF16),
        ],
        in_specs=[pl.BlockSpec(memory_space=pltpu.HBM)],
        out_specs=[vmem] * 3,
        scratch_shapes=[
            pltpu.VMEM((rows, 2 * HALF), F32),
            pltpu.VMEM((rows, 2 * HALF), BF16),
            pltpu.VMEM((rows, 2 * HALF), BF16),
            pltpu.VMEM((rows, HALF), F32),
            pltpu.VMEM((rows, HALF), F32),
            pltpu.VMEM((2, 2 * HALF, 2 * HALF), F32),
            pltpu.VMEM((2, sum(EARLY) * CHUNK, 2 * HALF), F32),
            pltpu.VMEM((2, 16, HALF), F32),
            pltpu.VMEM((2, 2, 16, HALF), F32),
            pltpu.VMEM((2, 2 * HALF, HALF), F32),
            pltpu.VMEM((n, size1 + 1, HALF), F32),
            pltpu.VMEM((n, size1 + 1, HALF), F32),
            pltpu.VMEM((n, size1, HALF), F32),
            pltpu.VMEM((n // 2, size2, HALF), F32),
            pltpu.VMEM((n, size2, HALF), F32),
            pltpu.VMEM((n // 2, size2, HALF), F32),
            pltpu.VMEM((2, 2 * HALF, HALF), F32),
            pltpu.VMEM((2, 2 * HALF, HALF), F32),
            pltpu.VMEM((2, HALF, HALF), F32),
            pltpu.VMEM((2, HALF, HALF), F32),
            dma((chunks,)),
            dma((4,)),
            dma((4,)),
            dma((2, 2)),
            dma((2, 2)),
            dma((2, 2 * chunks)),
        ],
        compiler_params=pltpu.CompilerParams(
            collective_id=0, has_side_effects=True, vmem_limit_bytes=40 << 20
        ),
    )(pltpu.with_memory_space_constraint(snapshots, pltpu.HBM))
    return pl.pallas_call(
        last,
        out_shape=jax.ShapeDtypeStruct((rows, 2 * HALF), F32),
        in_specs=[vmem] * 3,
        out_specs=pl.BlockSpec(memory_space=pltpu.HBM),
        scratch_shapes=[pltpu.VMEM((rows, 2 * HALF), F32), dma((chunks,))],
        compiler_params=pltpu.CompilerParams(vmem_limit_bytes=24 << 20),
    )(t2, b2, w)


def solution(mesh):
    return jax.shard_map(
        functools.partial(local, mesh.shape["row"], mesh.shape["col"]),
        mesh=mesh,
        in_specs=(P("row", "col"),),
        out_specs=P("row", "col"),
        check_vma=False,
    )
```

```python
import functools

import jax
import jax.numpy as jnp
from jax import lax
from jax.experimental import pallas as pl
from jax.experimental.pallas import tpu as pltpu
from jax.sharding import PartitionSpec as P

INNER_ROUNDS = 10
HALF = 128
CHUNK = 128
EARLY = (3,3)
SOLVE_ROWS = 64
MESH = pl.DeviceIdType.MESH
F32 = jnp.float32
BF16 = jnp.bfloat16


def split(value):
    high = value.astype(BF16)
    return high, (value - high.astype(F32)).astype(BF16)


def dot(left, right):
    return jnp.dot(left, right, preferred_element_type=F32)


def dot_rows(left, right):
    return lax.dot_general(left, right, (((0,), (0,)), ((), ())), preferred_element_type=F32)


def exact(left, right):
    return jnp.dot(left, right, precision=lax.Precision.HIGHEST, preferred_element_type=F32)


def exact_rows(left, right):
    return lax.dot_general(
        left, right, (((0,), (0,)), ((), ())), precision=lax.Precision.HIGHEST, preferred_element_type=F32
    )


def iota(shape, axis):
    return lax.broadcasted_iota(jnp.int32, shape, axis)


def reversal():
    return (iota((HALF, HALF), 0) + iota((HALF, HALF), 1) == HALF - 1).astype(F32)


def shifted(first, second, axis):
    place = iota(first.shape, axis)
    mixed = jnp.where(place == 0, first, second)
    new_first = jnp.where(place == HALF - 1, second, pltpu.roll(first, HALF - 1, axis))
    new_second = jnp.where(place == 0, second, pltpu.roll(mixed, 1, axis))
    return new_first, new_second


def angles(diag_first, diag_second, cross, turn):
    slot = iota((1, HALF), 1)
    upper = jnp.where(slot == 0, 2 * HALF - 1, jnp.where(turn >= slot, turn - slot, turn - slot + 2 * HALF - 1))
    lead = turn + slot < upper
    gap = diag_first - diag_second
    gap_lead = jnp.where(lead, gap, -gap)
    height = jnp.where(gap_lead >= 0, -2.0, 2.0) * cross
    width = jnp.abs(gap)
    big = jnp.maximum(width, jnp.abs(height))
    some = big > 0
    scale = 1.0 / jnp.where(some, big, 1.0)
    width, height = jnp.where(some, width * scale, 1.0), height * scale
    inverse = lax.rsqrt(width * width + height * height)
    squared = 0.5 + 0.5 * (width * inverse)
    inverse_cosine = lax.rsqrt(squared)
    cosine = squared * inverse_cosine
    sine = (0.5 * height * inverse) * inverse_cosine
    return cosine, jnp.where(lead, -sine, sine)


def fresh_basis(basis):
    basis[0] = (iota((2 * HALF, HALF), 0) == iota((2 * HALF, HALF), 1)).astype(F32)
    basis[1] = (iota((2 * HALF, HALF), 0) + iota((2 * HALF, HALF), 1) == 2 * HALF - 1).astype(F32)


def turn_columns(ref, where, cosine, factor):
    first, second = ref[0, where], ref[1, where]
    first, second = first * cosine + second * factor, second * cosine - first * factor
    first, second = shifted(first, second, 1)
    ref[0, where], ref[1, where] = first, second
    return first, second


def places():
    count = 2 * HALF - 1
    slot = iota((HALF, 2 * HALF), 0)
    natural = iota((HALF, 2 * HALF), 1)
    back = INNER_ROUNDS - slot
    place = jnp.where(slot == 0, count, jnp.where(back >= 0, back, back + count))
    return natural == slot + INNER_ROUNDS, natural == place


def natural_basis(basis):
    first_place, second_place = places()
    a, b = first_place.astype(BF16), second_place.astype(BF16)
    return tuple((dot(x, a) + dot(y, b)).astype(BF16) for x, y in zip(split(basis[0]), split(basis[1])))


def rebuild(turns, basis):
    fresh_basis(basis)

    def turn(index, carry):
        cosine, factor = turns[0, pl.ds(index, 1)], turns[1, pl.ds(index, 1)]
        for c in range(2 * HALF // SOLVE_ROWS):
            turn_columns(basis, pl.ds(c * SOLVE_ROWS, SOLVE_ROWS), cosine, factor)
        return carry

    lax.fori_loop(0, INNER_ROUNDS, turn, 0)
    return natural_basis(basis)


def solve(tt, tb, bb, basis, image, turns=None):
    fresh_basis(basis)
    image[0] = jnp.concatenate([tt, tb.T], 0)
    image[1] = exact(jnp.concatenate([tb, bb], 0), reversal())

    def product(left, right):
        return jnp.sum((left * right).reshape(-1, 8, HALF), axis=0)

    def over_rows(value):
        return jnp.sum(value, axis=0, keepdims=True)

    def turn(index, entries):
        diag_first, diag_second, cross = entries
        cosine, factor = angles(diag_first, diag_second, cross, index)
        if turns is not None:
            turns[0, pl.ds(index, 1)] = cosine
            turns[1, pl.ds(index, 1)] = factor
        found = None
        for c in range(2 * HALF // SOLVE_ROWS):
            where = pl.ds(c * SOLVE_ROWS, SOLVE_ROWS)
            v_first, _ = turn_columns(basis, where, cosine, factor)
            _, w_second = turn_columns(image, where, cosine, factor)
            part = product(v_first, w_second)
            found = part if found is None else found + part
        keep, take, mix = cosine * cosine, factor * factor, 2.0 * cosine * factor * cross
        diag_first, diag_second = shifted(
            keep * diag_first + take * diag_second + mix, keep * diag_second + take * diag_first - mix, 1
        )
        return diag_first, diag_second, over_rows(found)

    start = (
        over_rows(product(basis[0], image[0])),
        over_rows(product(basis[1], image[1])),
        over_rows(product(basis[0], image[1])),
    )
    lax.fori_loop(0, INNER_ROUNDS, turn, start)
    high, low = natural_basis(basis)

    def turned():
        a, b = (place.astype(F32) for place in places())
        placed = exact(image[0], a) + exact(image[1], b)
        upper = exact_rows(basis[0], placed)
        lower = exact_rows(basis[1], placed)

        def block(columns):
            left = slice(columns * HALF, (columns + 1) * HALF)
            return exact(a[:, left].T, upper[:, left]) + exact(b[:, left].T, lower[:, left])

        return block(0), block(1)

    return high, low, turned


def times_basis(high, low, basis_high, basis_low):
    return dot(high, basis_high) + dot(low, basis_high) + dot(high, basis_low)


class Peers:
    def __init__(self, n):
        self.n, self.half = n, n // 2
        self.me = lax.axis_index("row")
        self.group, self.place = self.me // self.half, lax.rem(self.me, self.half)

    def at(self, other, offset):
        return lax.rem(self.group + other, 2) * self.half + lax.rem(self.place + self.half + offset, self.half)

    def each(self, action):
        def step(k, carry):
            offset = self.half // 2 + (1 - 2 * lax.rem(k, 2)) * ((k + 1) // 2)
            action(self.at(1, offset))
            action(self.at(0, offset))
            return carry

        lax.fori_loop(0, self.half - 1, step, 0)
        action(self.at(1, 0))

    def near(self, action):
        quarter = self.half // 4
        offsets = range(quarter - self.half // 2 + 1, quarter + 1)
        for offset in sorted(offsets, key=abs, reverse=True):
            action(self.at(1, offset))
            if offset:
                action(self.at(0, offset))


class Sum:
    def __init__(self, mine, parts, total, sems, peers, copies):
        self.mine, self.parts, self.total, self.sems, self.peers, self.copies = mine, parts, total, sems, peers, copies
        self.me = peers.me
        self.slices = peers.n // copies

    def slice_of(self, peer):
        if self.copies == 1:
            return peer
        half = self.peers.half
        return (peer // half) * (half // 2) + lax.rem(lax.rem(peer, half), half // 2)

    def drain(self, source, count, index):
        view = source.at[pl.ds(0, count)]
        pltpu.make_async_copy(view, view, self.sems.at[index]).wait()

    def scatter(self):
        self.peers.each(
            lambda peer: pltpu.make_async_remote_copy(
                src_ref=self.mine.at[self.slice_of(peer)],
                dst_ref=self.parts.at[self.me],
                send_sem=self.sems.at[0],
                recv_sem=self.sems.at[1],
                device_id={"row": peer},
                device_id_type=MESH,
            ).start()
        )
        self.parts[self.me] = self.mine[self.slice_of(self.me)]

    def add(self):
        self.drain(self.parts, self.peers.n - 1, 1)
        total = self.parts[0]
        for i in range(1, self.peers.n):
            total = total + self.parts[i]
        return total

    def gather(self, piece):
        own = self.slice_of(self.me)
        self.total[own] = piece
        (self.peers.each if self.copies == 1 else self.peers.near)(
            lambda peer: pltpu.make_async_remote_copy(
                src_ref=self.total.at[own],
                dst_ref=self.total.at[own],
                send_sem=self.sems.at[2],
                recv_sem=self.sems.at[3],
                device_id={"row": peer},
                device_id_type=MESH,
            ).start()
        )

    def wait(self):
        self.drain(self.total, self.slices - 1, 3)

    def finish(self):
        self.drain(self.parts, self.peers.n - 1, 0)
        self.drain(self.total, self.slices - 1, 2)


def kernel(
    n, cycle, x_hbm, high_ref, low_ref, w_ref,
    x, t2, b2, xh, xl, left, right, gram, got_rows, turns, got_turns, other,
    mine1, parts1, total1, mine2, parts2, total2,
    basis, image, blocks, got_blocks,
    load_sems, sums1, sums2, block_sems, turn_sems, chunk_sems,
):
    col = lax.axis_index("col")
    chunks = x.shape[0] // CHUNK
    is_head, is_tail = col == 0, col == cycle - 1

    def load(c):
        where = pl.ds(c * CHUNK, CHUNK)
        return pltpu.make_async_copy(x_hbm.at[where], x.at[where], load_sems.at[c])

    for c in range(chunks):
        load(c).start()

    barrier = pltpu.get_barrier_semaphore()

    peers = Peers(n)
    peers.each(lambda peer: pl.semaphore_signal(barrier, inc=1, device_id={"row": peer}, device_id_type=MESH))

    @pl.when(jnp.logical_not(is_tail))
    def _():
        pl.semaphore_signal(barrier, inc=1, device_id={"col": col + 1}, device_id_type=MESH)

    @pl.when(jnp.logical_not(is_head))
    def _():
        pl.semaphore_signal(barrier, inc=1, device_id={"col": col - 1}, device_id_type=MESH)

    gram[...] = jnp.zeros_like(gram)
    for c in range(chunks):
        load(c).wait()
        where = pl.ds(c * CHUNK, CHUNK)
        high, low = split(x[where])
        xh[where] = high
        xl[where] = low
        gram[0] += dot_rows(high, high) + dot_rows(low, low)
        gram[1] += dot_rows(high, low)
    full = gram[0] + (gram[1] + gram[1].T)
    tt, tb, bb = full[:HALF, :HALF], full[:HALF, HALF:], full[HALF:, HALF:]
    below = iota((HALF, HALF), 0) >= iota((HALF, HALF), 1)
    eye = iota((HALF, HALF), 0) == iota((HALF, HALF), 1)
    folded = jnp.where(below, tt, bb)
    size1 = 2 * HALF // n
    mine1[:, :size1] = jnp.concatenate([tb, folded], 0).reshape(n, size1, HALF)
    corner = jnp.sum(jnp.where(eye, bb, 0.0), axis=0, keepdims=True)
    mine1[:, size1:] = jnp.broadcast_to(corner[None], (n, 1, HALF))

    inner = jnp.logical_not(jnp.logical_or(is_head, is_tail))

    @pl.when(inner)
    def _():
        pl.semaphore_wait(barrier, n + 1)

    @pl.when(jnp.logical_not(inner))
    def _():
        pl.semaphore_wait(barrier, n)

    def transfer(kind, source, target, sems, index):
        return pltpu.make_async_remote_copy(
            src_ref=source,
            dst_ref=target,
            send_sem=sems.at[0, index],
            recv_sem=sems.at[1, index],
            device_id={"col": col + 1 if kind == 0 else col - 1},
            device_id_type=MESH,
        )

    early = sum(EARLY)

    def rows_move(kind, c):
        where = pl.ds(c * CHUNK, CHUNK)
        if c < early:
            source, target = x.at[where], got_rows.at[kind, where]
        else:
            source, target = (left if kind else right).at[where], (b2 if kind else t2).at[where]
        return transfer(kind, source, target, chunk_sems, kind * chunks + c)

    def block_move(kind):
        return transfer(kind, blocks.at[kind], got_blocks.at[kind], block_sems, kind)

    def turn_move(kind):
        return transfer(kind, turns, got_turns.at[kind], turn_sems, kind)

    def start(move):
        @pl.when(jnp.logical_not(is_tail))
        def _():
            move(0).start()

        @pl.when(jnp.logical_not(is_head))
        def _():
            move(1).start()

    def arrive(move):
        @pl.when(jnp.logical_not(is_head))
        def _():
            move(0).wait_recv()

        @pl.when(jnp.logical_not(is_tail))
        def _():
            move(1).wait_recv()

    def sent(move):
        @pl.when(jnp.logical_not(is_tail))
        def _():
            move(0).wait_send()

        @pl.when(jnp.logical_not(is_head))
        def _():
            move(1).wait_send()

    def rows(c):
        return lambda kind: rows_move(kind, c)

    sum1 = Sum(mine1, parts1, total1, sums1, peers, 1)
    sum1.scatter()
    for c in range(EARLY[0]):
        start(rows(c))
    piece = sum1.add()
    corner = piece[size1:]
    sum1.gather(piece[:size1])
    for c in range(EARLY[0], early):
        start(rows(c))

    @pl.when(is_head)
    def _():
        got_rows[0] = x[: early * CHUNK]

    @pl.when(is_tail)
    def _():
        got_rows[1] = x[: early * CHUNK]

    sum1.wait()
    whole = total1[...].reshape(2 * HALF, HALF)
    tb, folded = whole[:HALF], whole[HALF:]
    turned_fold = folded.T
    tt = jnp.where(below, folded, turned_fold)
    bb = jnp.where(below, turned_fold, folded)
    bb = jnp.where(eye, jnp.broadcast_to(corner, (HALF, HALF)), bb)

    turns[...] = jnp.zeros_like(turns)
    basis_high, basis_low, turned = solve(tt, tb, bb, basis, image, turns)

    start(turn_move)

    @pl.when(is_head)
    def _():
        got_turns[0] = turns[...]

    @pl.when(is_tail)
    def _():
        got_turns[1] = turns[...]

    for c in range(early, chunks):
        where = pl.ds(c * CHUNK, CHUNK)
        moved = times_basis(xh[where], xl[where], basis_high, basis_low)
        top, bottom = moved[:, :HALF], moved[:, HALF:]
        right[where] = jnp.where(is_head, bottom, top)
        left[where] = bottom

        @pl.when(is_head)
        def _():
            t2[where] = top

        @pl.when(is_tail)
        def _():
            b2[where] = top

        start(rows(c))

    tt, bb = turned()
    blocks[0] = jnp.where(is_head, bb, tt)
    blocks[1] = bb

    @pl.when(is_head)
    def _():
        got_blocks[0] = tt

    @pl.when(is_tail)
    def _():
        got_blocks[1] = tt

    arrive(turn_move)
    got_top = [
        jnp.where(col == 1, part[:, HALF:], part[:, :HALF]) for part in rebuild(got_turns.at[0], other)
    ]
    got_bottom = [
        jnp.where(is_tail, part[:, :HALF], part[:, HALF:]) for part in rebuild(got_turns.at[1], other)
    ]
    for c in range(early):
        arrive(rows(c))
    cross = jnp.zeros((HALF, HALF), F32)
    for c in range(chunks):
        where = pl.ds(c * CHUNK, CHUNK)
        if c < early:
            t2[where] = times_basis(*split(got_rows[0, where]), *got_top)
            b2[where] = times_basis(*split(got_rows[1, where]), *got_bottom)
        else:
            arrive(rows(c))
        th, tl = split(t2[where])
        bh, bl = split(b2[where])
        high_ref[where, :HALF], high_ref[where, HALF:] = th, bh
        low_ref[where, :HALF], low_ref[where, HALF:] = tl, bl
        cross += dot_rows(th, bh) + dot_rows(tl, bh) + dot_rows(th, bl)
    mine2[...] = cross.reshape(mine2.shape)
    sum2 = Sum(mine2, parts2, total2, sums2, peers, 2)
    sum2.scatter()
    start(block_move)
    sum2.gather(sum2.add())
    arrive(block_move)
    sum2.wait()
    tb = total2[...].reshape(HALF, HALF)
    basis_high, basis_low, _ = solve(got_blocks[0], tb, got_blocks[1], basis, image)
    w_ref[0] = basis_high
    w_ref[1] = basis_low

    sum1.finish()
    sum2.finish()
    for c in range(chunks):
        sent(rows(c))
    sent(block_move)
    sent(turn_move)


def last(high_ref, low_ref, w_ref, out, held, sems):
    chunks = held.shape[0] // CHUNK

    def store(c):
        where = pl.ds(c * CHUNK, CHUNK)
        return pltpu.make_async_copy(held.at[where], out.at[where], sems.at[c])

    for c in range(chunks):
        where = pl.ds(c * CHUNK, CHUNK)
        held[where] = times_basis(high_ref[where], low_ref[where], w_ref[0], w_ref[1])
        store(c).start()
    for c in range(chunks):
        store(c).wait()


def local(n, cycle, snapshots):
    rows = snapshots.shape[0]
    chunks = rows // CHUNK
    dma = pltpu.SemaphoreType.DMA
    vmem = pl.BlockSpec(memory_space=pltpu.VMEM)
    size1, size2 = 2 * HALF // n, 2 * HALF // n
    high, low, w = pl.pallas_call(
        functools.partial(kernel, n, cycle),
        out_shape=[
            jax.ShapeDtypeStruct((rows, 2 * HALF), BF16),
            jax.ShapeDtypeStruct((rows, 2 * HALF), BF16),
            jax.ShapeDtypeStruct((2, 2 * HALF, 2 * HALF), BF16),
        ],
        in_specs=[pl.BlockSpec(memory_space=pltpu.HBM)],
        out_specs=[vmem] * 3,
        scratch_shapes=[
            pltpu.VMEM((rows, 2 * HALF), F32),
            pltpu.VMEM((rows, HALF), F32),
            pltpu.VMEM((rows, HALF), F32),
            pltpu.VMEM((rows, 2 * HALF), BF16),
            pltpu.VMEM((rows, 2 * HALF), BF16),
            pltpu.VMEM((rows, HALF), F32),
            pltpu.VMEM((rows, HALF), F32),
            pltpu.VMEM((2, 2 * HALF, 2 * HALF), F32),
            pltpu.VMEM((2, sum(EARLY) * CHUNK, 2 * HALF), F32),
            pltpu.VMEM((2, 16, HALF), F32),
            pltpu.VMEM((2, 2, 16, HALF), F32),
            pltpu.VMEM((2, 2 * HALF, HALF), F32),
            pltpu.VMEM((n, size1 + 1, HALF), F32),
            pltpu.VMEM((n, size1 + 1, HALF), F32),
            pltpu.VMEM((n, size1, HALF), F32),
            pltpu.VMEM((n // 2, size2, HALF), F32),
            pltpu.VMEM((n, size2, HALF), F32),
            pltpu.VMEM((n // 2, size2, HALF), F32),
            pltpu.VMEM((2, 2 * HALF, HALF), F32),
            pltpu.VMEM((2, 2 * HALF, HALF), F32),
            pltpu.VMEM((2, HALF, HALF), F32),
            pltpu.VMEM((2, HALF, HALF), F32),
            dma((chunks,)),
            dma((4,)),
            dma((4,)),
            dma((2, 2)),
            dma((2, 2)),
            dma((2, 2 * chunks)),
        ],
        compiler_params=pltpu.CompilerParams(
            collective_id=0, has_side_effects=True, vmem_limit_bytes=40 << 20
        ),
    )(pltpu.with_memory_space_constraint(snapshots, pltpu.HBM))
    return pl.pallas_call(
        last,
        out_shape=jax.ShapeDtypeStruct((rows, 2 * HALF), F32),
        in_specs=[vmem] * 3,
        out_specs=pl.BlockSpec(memory_space=pltpu.HBM),
        scratch_shapes=[pltpu.VMEM((rows, 2 * HALF), F32), dma((chunks,))],
        compiler_params=pltpu.CompilerParams(vmem_limit_bytes=24 << 20),
    )(high, low, w)


def solution(mesh):
    return jax.shard_map(
        functools.partial(local, mesh.shape["row"], mesh.shape["col"]),
        mesh=mesh,
        in_specs=(P("row", "col"),),
        out_specs=P("row", "col"),
        check_vma=False,
    )
```

```python
import functools

import jax
import jax.numpy as jnp
from jax import lax
from jax.experimental import pallas as pl
from jax.experimental.pallas import tpu as pltpu
from jax.sharding import PartitionSpec as P

INNER_ROUNDS = 10
HALF = 128
CHUNK = 128
EARLY = (4,2)
SOLVE_ROWS = 64
MESH = pl.DeviceIdType.MESH
F32 = jnp.float32
BF16 = jnp.bfloat16


def split(value):
    high = value.astype(BF16)
    return high, (value - high.astype(F32)).astype(BF16)


def dot(left, right):
    return jnp.dot(left, right, preferred_element_type=F32)


def dot_rows(left, right):
    return lax.dot_general(left, right, (((0,), (0,)), ((), ())), preferred_element_type=F32)


def exact(left, right):
    return jnp.dot(left, right, precision=lax.Precision.HIGHEST, preferred_element_type=F32)


def exact_rows(left, right):
    return lax.dot_general(
        left, right, (((0,), (0,)), ((), ())), precision=lax.Precision.HIGHEST, preferred_element_type=F32
    )


def iota(shape, axis):
    return lax.broadcasted_iota(jnp.int32, shape, axis)


def reversal():
    return (iota((HALF, HALF), 0) + iota((HALF, HALF), 1) == HALF - 1).astype(F32)


def shifted(first, second, axis):
    place = iota(first.shape, axis)
    mixed = jnp.where(place == 0, first, second)
    new_first = jnp.where(place == HALF - 1, second, pltpu.roll(first, HALF - 1, axis))
    new_second = jnp.where(place == 0, second, pltpu.roll(mixed, 1, axis))
    return new_first, new_second


def angles(diag_first, diag_second, cross, turn):
    slot = iota((1, HALF), 1)
    upper = jnp.where(slot == 0, 2 * HALF - 1, jnp.where(turn >= slot, turn - slot, turn - slot + 2 * HALF - 1))
    lead = turn + slot < upper
    gap = diag_first - diag_second
    gap_lead = jnp.where(lead, gap, -gap)
    height = jnp.where(gap_lead >= 0, -2.0, 2.0) * cross
    width = jnp.abs(gap)
    big = jnp.maximum(width, jnp.abs(height))
    some = big > 0
    scale = 1.0 / jnp.where(some, big, 1.0)
    width, height = jnp.where(some, width * scale, 1.0), height * scale
    inverse = lax.rsqrt(width * width + height * height)
    squared = 0.5 + 0.5 * (width * inverse)
    inverse_cosine = lax.rsqrt(squared)
    cosine = squared * inverse_cosine
    sine = (0.5 * height * inverse) * inverse_cosine
    return cosine, jnp.where(lead, -sine, sine)


def fresh_basis(basis):
    basis[0] = (iota((2 * HALF, HALF), 0) == iota((2 * HALF, HALF), 1)).astype(F32)
    basis[1] = (iota((2 * HALF, HALF), 0) + iota((2 * HALF, HALF), 1) == 2 * HALF - 1).astype(F32)


def turn_columns(ref, where, cosine, factor):
    first, second = ref[0, where], ref[1, where]
    first, second = first * cosine + second * factor, second * cosine - first * factor
    first, second = shifted(first, second, 1)
    ref[0, where], ref[1, where] = first, second
    return first, second


def places():
    count = 2 * HALF - 1
    slot = iota((HALF, 2 * HALF), 0)
    natural = iota((HALF, 2 * HALF), 1)
    back = INNER_ROUNDS - slot
    place = jnp.where(slot == 0, count, jnp.where(back >= 0, back, back + count))
    return natural == slot + INNER_ROUNDS, natural == place


def natural_basis(basis):
    first_place, second_place = places()
    a, b = first_place.astype(BF16), second_place.astype(BF16)
    return tuple((dot(x, a) + dot(y, b)).astype(BF16) for x, y in zip(split(basis[0]), split(basis[1])))


def rebuild(turns, basis):
    fresh_basis(basis)

    def turn(index, carry):
        cosine, factor = turns[0, pl.ds(index, 1)], turns[1, pl.ds(index, 1)]
        for c in range(2 * HALF // SOLVE_ROWS):
            turn_columns(basis, pl.ds(c * SOLVE_ROWS, SOLVE_ROWS), cosine, factor)
        return carry

    lax.fori_loop(0, INNER_ROUNDS, turn, 0)
    return natural_basis(basis)


def prepare(tt, bb, basis, image):
    fresh_basis(basis)
    image[0, :HALF] = tt
    image[1, HALF:] = exact(bb, reversal())


def solve(tb, basis, image, turns=None):
    image[0, HALF:] = tb.T
    image[1, :HALF] = exact(tb, reversal())

    def product(left, right):
        return jnp.sum((left * right).reshape(-1, 8, HALF), axis=0)

    def over_rows(value):
        return jnp.sum(value, axis=0, keepdims=True)

    def turn(index, entries):
        diag_first, diag_second, cross = entries
        cosine, factor = angles(diag_first, diag_second, cross, index)
        if turns is not None:
            turns[0, pl.ds(index, 1)] = cosine
            turns[1, pl.ds(index, 1)] = factor
        found = None
        for c in range(2 * HALF // SOLVE_ROWS):
            where = pl.ds(c * SOLVE_ROWS, SOLVE_ROWS)
            v_first, _ = turn_columns(basis, where, cosine, factor)
            _, w_second = turn_columns(image, where, cosine, factor)
            part = product(v_first, w_second)
            found = part if found is None else found + part
        keep, take, mix = cosine * cosine, factor * factor, 2.0 * cosine * factor * cross
        diag_first, diag_second = shifted(
            keep * diag_first + take * diag_second + mix, keep * diag_second + take * diag_first - mix, 1
        )
        return diag_first, diag_second, over_rows(found)

    start = (
        over_rows(product(basis[0], image[0])),
        over_rows(product(basis[1], image[1])),
        over_rows(product(basis[0], image[1])),
    )
    lax.fori_loop(0, INNER_ROUNDS, turn, start)
    high, low = natural_basis(basis)

    def turned():
        a, b = (place.astype(F32) for place in places())
        placed = exact(image[0], a) + exact(image[1], b)
        upper = exact_rows(basis[0], placed)
        lower = exact_rows(basis[1], placed)

        def block(columns):
            left = slice(columns * HALF, (columns + 1) * HALF)
            return exact(a[:, left].T, upper[:, left]) + exact(b[:, left].T, lower[:, left])

        return block(0), block(1)

    return high, low, turned


def times_basis(high, low, basis_high, basis_low):
    return dot(high, basis_high) + dot(low, basis_high) + dot(high, basis_low)


class Peers:
    def __init__(self, n):
        self.n, self.half = n, n // 2
        self.me = lax.axis_index("row")
        self.group, self.place = self.me // self.half, lax.rem(self.me, self.half)

    def at(self, other, offset):
        return lax.rem(self.group + other, 2) * self.half + lax.rem(self.place + self.half + offset, self.half)

    def each(self, action):
        def step(k, carry):
            offset = self.half // 2 + (1 - 2 * lax.rem(k, 2)) * ((k + 1) // 2)
            action(self.at(1, offset))
            action(self.at(0, offset))
            return carry

        lax.fori_loop(0, self.half - 1, step, 0)
        action(self.at(1, 0))

    def near(self, action):
        quarter = self.half // 4
        offsets = range(quarter - self.half // 2 + 1, quarter + 1)
        for offset in sorted(offsets, key=abs, reverse=True):
            action(self.at(1, offset))
            if offset:
                action(self.at(0, offset))


class Sum:
    def __init__(self, mine, parts, total, sems, peers, copies):
        self.mine, self.parts, self.total, self.sems, self.peers, self.copies = mine, parts, total, sems, peers, copies
        self.me = peers.me
        self.slices = peers.n // copies

    def slice_of(self, peer):
        if self.copies == 1:
            return peer
        half = self.peers.half
        return (peer // half) * (half // 2) + lax.rem(lax.rem(peer, half), half // 2)

    def drain(self, source, count, index):
        view = source.at[pl.ds(0, count)]
        pltpu.make_async_copy(view, view, self.sems.at[index]).wait()

    def scatter(self):
        self.peers.each(
            lambda peer: pltpu.make_async_remote_copy(
                src_ref=self.mine.at[self.slice_of(peer)],
                dst_ref=self.parts.at[self.me],
                send_sem=self.sems.at[0],
                recv_sem=self.sems.at[1],
                device_id={"row": peer},
                device_id_type=MESH,
            ).start()
        )
        self.parts[self.me] = self.mine[self.slice_of(self.me)]

    def add(self):
        self.drain(self.parts, self.peers.n - 1, 1)
        total = self.parts[0]
        for i in range(1, self.peers.n):
            total = total + self.parts[i]
        return total

    def gather(self, piece):
        own = self.slice_of(self.me)
        self.total[own] = piece
        (self.peers.each if self.copies == 1 else self.peers.near)(
            lambda peer: pltpu.make_async_remote_copy(
                src_ref=self.total.at[own],
                dst_ref=self.total.at[own],
                send_sem=self.sems.at[2],
                recv_sem=self.sems.at[3],
                device_id={"row": peer},
                device_id_type=MESH,
            ).start()
        )

    def wait(self):
        self.drain(self.total, self.slices - 1, 3)

    def finish(self):
        self.drain(self.parts, self.peers.n - 1, 0)
        self.drain(self.total, self.slices - 1, 2)


def kernel(
    n, cycle, x_hbm, high_ref, low_ref, w_ref,
    x, t2, b2, xh, xl, left, right, gram, got_rows, turns, got_turns, other,
    mine1, parts1, total1, mine2, parts2, total2,
    basis, image, blocks, got_blocks,
    load_sems, sums1, sums2, block_sems, turn_sems, chunk_sems,
):
    col = lax.axis_index("col")
    chunks = x.shape[0] // CHUNK
    is_head, is_tail = col == 0, col == cycle - 1

    def load(c):
        where = pl.ds(c * CHUNK, CHUNK)
        return pltpu.make_async_copy(x_hbm.at[where], x.at[where], load_sems.at[c])

    for c in range(chunks):
        load(c).start()

    barrier = pltpu.get_barrier_semaphore()

    peers = Peers(n)
    peers.each(lambda peer: pl.semaphore_signal(barrier, inc=1, device_id={"row": peer}, device_id_type=MESH))

    @pl.when(jnp.logical_not(is_tail))
    def _():
        pl.semaphore_signal(barrier, inc=1, device_id={"col": col + 1}, device_id_type=MESH)

    @pl.when(jnp.logical_not(is_head))
    def _():
        pl.semaphore_signal(barrier, inc=1, device_id={"col": col - 1}, device_id_type=MESH)

    gram[...] = jnp.zeros_like(gram)
    for c in range(chunks):
        load(c).wait()
        where = pl.ds(c * CHUNK, CHUNK)
        high, low = split(x[where])
        xh[where] = high
        xl[where] = low
        gram[0] += dot_rows(high, high) + dot_rows(low, low)
        gram[1] += dot_rows(high, low)
    full = gram[0] + (gram[1] + gram[1].T)
    tt, tb, bb = full[:HALF, :HALF], full[:HALF, HALF:], full[HALF:, HALF:]
    below = iota((HALF, HALF), 0) >= iota((HALF, HALF), 1)
    eye = iota((HALF, HALF), 0) == iota((HALF, HALF), 1)
    folded = jnp.where(below, tt, bb)
    size1 = 2 * HALF // n
    mine1[:, :size1] = jnp.concatenate([tb, folded], 0).reshape(n, size1, HALF)
    corner = jnp.sum(jnp.where(eye, bb, 0.0), axis=0, keepdims=True)
    mine1[:, size1:] = jnp.broadcast_to(corner[None], (n, 1, HALF))

    inner = jnp.logical_not(jnp.logical_or(is_head, is_tail))

    @pl.when(inner)
    def _():
        pl.semaphore_wait(barrier, n + 1)

    @pl.when(jnp.logical_not(inner))
    def _():
        pl.semaphore_wait(barrier, n)

    def transfer(kind, source, target, sems, index):
        return pltpu.make_async_remote_copy(
            src_ref=source,
            dst_ref=target,
            send_sem=sems.at[0, index],
            recv_sem=sems.at[1, index],
            device_id={"col": col + 1 if kind == 0 else col - 1},
            device_id_type=MESH,
        )

    early = sum(EARLY)

    def rows_move(kind, c):
        where = pl.ds(c * CHUNK, CHUNK)
        if c < early:
            source, target = x.at[where], got_rows.at[kind, where]
        else:
            source, target = (left if kind else right).at[where], (b2 if kind else t2).at[where]
        return transfer(kind, source, target, chunk_sems, kind * chunks + c)

    def block_move(kind):
        return transfer(kind, blocks.at[kind], got_blocks.at[kind], block_sems, kind)

    def turn_move(kind):
        return transfer(kind, turns, got_turns.at[kind], turn_sems, kind)

    def start(move):
        @pl.when(jnp.logical_not(is_tail))
        def _():
            move(0).start()

        @pl.when(jnp.logical_not(is_head))
        def _():
            move(1).start()

    def arrive(move):
        @pl.when(jnp.logical_not(is_head))
        def _():
            move(0).wait_recv()

        @pl.when(jnp.logical_not(is_tail))
        def _():
            move(1).wait_recv()

    def sent(move):
        @pl.when(jnp.logical_not(is_tail))
        def _():
            move(0).wait_send()

        @pl.when(jnp.logical_not(is_head))
        def _():
            move(1).wait_send()

    def rows(c):
        return lambda kind: rows_move(kind, c)

    sum1 = Sum(mine1, parts1, total1, sums1, peers, 1)
    sum1.scatter()
    for c in range(EARLY[0]):
        start(rows(c))
    piece = sum1.add()
    corner = piece[size1:]
    sum1.gather(piece[:size1])
    for c in range(EARLY[0], early):
        start(rows(c))

    @pl.when(is_head)
    def _():
        got_rows[0] = x[: early * CHUNK]

    @pl.when(is_tail)
    def _():
        got_rows[1] = x[: early * CHUNK]

    sum1.wait()
    whole = total1[...].reshape(2 * HALF, HALF)
    tb, folded = whole[:HALF], whole[HALF:]
    turned_fold = folded.T
    tt = jnp.where(below, folded, turned_fold)
    bb = jnp.where(below, turned_fold, folded)
    bb = jnp.where(eye, jnp.broadcast_to(corner, (HALF, HALF)), bb)

    turns[...] = jnp.zeros_like(turns)
    prepare(tt, bb, basis, image)
    basis_high, basis_low, turned = solve(tb, basis, image, turns)

    start(turn_move)

    @pl.when(is_head)
    def _():
        got_turns[0] = turns[...]

    @pl.when(is_tail)
    def _():
        got_turns[1] = turns[...]

    for c in range(early, chunks):
        where = pl.ds(c * CHUNK, CHUNK)
        moved = times_basis(xh[where], xl[where], basis_high, basis_low)
        top, bottom = moved[:, :HALF], moved[:, HALF:]
        right[where] = jnp.where(is_head, bottom, top)
        left[where] = bottom

        @pl.when(is_head)
        def _():
            t2[where] = top

        @pl.when(is_tail)
        def _():
            b2[where] = top

        start(rows(c))

    tt, bb = turned()
    blocks[0] = jnp.where(is_head, bb, tt)
    blocks[1] = bb

    @pl.when(is_head)
    def _():
        got_blocks[0] = tt

    @pl.when(is_tail)
    def _():
        got_blocks[1] = tt

    arrive(turn_move)
    got_top = [
        jnp.where(col == 1, part[:, HALF:], part[:, :HALF]) for part in rebuild(got_turns.at[0], other)
    ]
    got_bottom = [
        jnp.where(is_tail, part[:, :HALF], part[:, HALF:]) for part in rebuild(got_turns.at[1], other)
    ]
    for c in range(early):
        arrive(rows(c))
    cross = jnp.zeros((HALF, HALF), F32)
    for c in range(chunks):
        where = pl.ds(c * CHUNK, CHUNK)
        if c < early:
            t2[where] = times_basis(*split(got_rows[0, where]), *got_top)
            b2[where] = times_basis(*split(got_rows[1, where]), *got_bottom)
        else:
            arrive(rows(c))
        th, tl = split(t2[where])
        bh, bl = split(b2[where])
        high_ref[where, :HALF], high_ref[where, HALF:] = th, bh
        low_ref[where, :HALF], low_ref[where, HALF:] = tl, bl
        cross += dot_rows(th, bh) + dot_rows(tl, bh) + dot_rows(th, bl)
    mine2[...] = cross.reshape(mine2.shape)
    sum2 = Sum(mine2, parts2, total2, sums2, peers, 2)
    sum2.scatter()
    start(block_move)
    sum2.gather(sum2.add())
    arrive(block_move)
    prepare(got_blocks[0], got_blocks[1], basis, image)
    sum2.wait()
    tb = total2[...].reshape(HALF, HALF)
    basis_high, basis_low, _ = solve(tb, basis, image)
    w_ref[0] = basis_high
    w_ref[1] = basis_low

    sum1.finish()
    sum2.finish()
    for c in range(chunks):
        sent(rows(c))
    sent(block_move)
    sent(turn_move)


def last(high_ref, low_ref, w_ref, out, held, sems):
    chunks = held.shape[0] // CHUNK

    def store(c):
        where = pl.ds(c * CHUNK, CHUNK)
        return pltpu.make_async_copy(held.at[where], out.at[where], sems.at[c])

    for c in range(chunks):
        where = pl.ds(c * CHUNK, CHUNK)
        held[where] = times_basis(high_ref[where], low_ref[where], w_ref[0], w_ref[1])
        store(c).start()
    for c in range(chunks):
        store(c).wait()


def local(n, cycle, snapshots):
    rows = snapshots.shape[0]
    chunks = rows // CHUNK
    dma = pltpu.SemaphoreType.DMA
    vmem = pl.BlockSpec(memory_space=pltpu.VMEM)
    size1, size2 = 2 * HALF // n, 2 * HALF // n
    high, low, w = pl.pallas_call(
        functools.partial(kernel, n, cycle),
        out_shape=[
            jax.ShapeDtypeStruct((rows, 2 * HALF), BF16),
            jax.ShapeDtypeStruct((rows, 2 * HALF), BF16),
            jax.ShapeDtypeStruct((2, 2 * HALF, 2 * HALF), BF16),
        ],
        in_specs=[pl.BlockSpec(memory_space=pltpu.HBM)],
        out_specs=[vmem] * 3,
        scratch_shapes=[
            pltpu.VMEM((rows, 2 * HALF), F32),
            pltpu.VMEM((rows, HALF), F32),
            pltpu.VMEM((rows, HALF), F32),
            pltpu.VMEM((rows, 2 * HALF), BF16),
            pltpu.VMEM((rows, 2 * HALF), BF16),
            pltpu.VMEM((rows, HALF), F32),
            pltpu.VMEM((rows, HALF), F32),
            pltpu.VMEM((2, 2 * HALF, 2 * HALF), F32),
            pltpu.VMEM((2, sum(EARLY) * CHUNK, 2 * HALF), F32),
            pltpu.VMEM((2, 16, HALF), F32),
            pltpu.VMEM((2, 2, 16, HALF), F32),
            pltpu.VMEM((2, 2 * HALF, HALF), F32),
            pltpu.VMEM((n, size1 + 1, HALF), F32),
            pltpu.VMEM((n, size1 + 1, HALF), F32),
            pltpu.VMEM((n, size1, HALF), F32),
            pltpu.VMEM((n // 2, size2, HALF), F32),
            pltpu.VMEM((n, size2, HALF), F32),
            pltpu.VMEM((n // 2, size2, HALF), F32),
            pltpu.VMEM((2, 2 * HALF, HALF), F32),
            pltpu.VMEM((2, 2 * HALF, HALF), F32),
            pltpu.VMEM((2, HALF, HALF), F32),
            pltpu.VMEM((2, HALF, HALF), F32),
            dma((chunks,)),
            dma((4,)),
            dma((4,)),
            dma((2, 2)),
            dma((2, 2)),
            dma((2, 2 * chunks)),
        ],
        compiler_params=pltpu.CompilerParams(
            collective_id=0, has_side_effects=True, vmem_limit_bytes=40 << 20
        ),
    )(pltpu.with_memory_space_constraint(snapshots, pltpu.HBM))
    return pl.pallas_call(
        last,
        out_shape=jax.ShapeDtypeStruct((rows, 2 * HALF), F32),
        in_specs=[vmem] * 3,
        out_specs=pl.BlockSpec(memory_space=pltpu.HBM),
        scratch_shapes=[pltpu.VMEM((rows, 2 * HALF), F32), dma((chunks,))],
        compiler_params=pltpu.CompilerParams(vmem_limit_bytes=24 << 20),
    )(high, low, w)


def solution(mesh):
    return jax.shard_map(
        functools.partial(local, mesh.shape["row"], mesh.shape["col"]),
        mesh=mesh,
        in_specs=(P("row", "col"),),
        out_specs=P("row", "col"),
        check_vma=False,
    )
```
